128 devices in a mesh: grp: 2 (over z_hi), lon: 8 (over x, core), lat: 8 (over y, z_lo).
Axes of the slice: x: 4, y: 4, z: 4 (z_hi: 2, z_lo: 2; z = z_hi * 2 + z_lo), core: 2. Of those that a mesh axis runs over, the one named last changes fastest.
Arguments:
- tracer: float32 [2, 6, 8, 256, 1024], P('grp', None, None, 'lon', 'lat'), may hold values from -6 to 6
- velocity: float32 [2, 2, 8, 256, 1024], P('grp', None, None, 'lon', 'lat'), may hold values from -0.2 to 0.2
- mixing: float32 [2, 8], P('grp'), may hold values from 0.03 to 0.12
- vertical_mixing: float32 [2, 8], P('grp'), may hold values from 0.03 to 0.12
- transfer_coef: float32 [256, 1024], P('lon', 'lat'), may hold values from 0.05 to 0.5
- land_mask: int32 [256, 1024], P('lon', 'lat'), may hold values from 0 to 1, as said below
Outputs:
- advanced: float32 [2, 6, 8, 256, 1024], P('grp', None, None, 'lon', 'lat')
The draws below stay inside these ranges and needn't reach their ends.
Inputs may be any that keep to these rules, and one draw needn't show every extreme that they name: `land_mask`: the share of ocean columns differs from block to block of 32 x 128 columns.
All inputs are finite; a program needn't handle non-finite values.
Results may differ from the reference program's by a relative error of at most 0.00002.
Values sent between devices are 32-bit elements; how exact they have to be, the bound alone decides.
A program may use at most 64 MiB of HBM per device.

```python
import math
import jax
import jax.numpy as jnp
from jax import lax

TRACERS = 6
LEVELS = 8
CX = 32
CY = 128
SUBSTEPS = 4
NX = 256
NY = 1024


def draw_land_mask(key, part):
    first_key, second_key = jax.random.split(jax.random.fold_in(key, 11))
    levels_block = jax.random.randint(first_key, (NX // CX, NY // CY), 1, 9)
    cell_draw = jax.random.randint(second_key, (NX, NY), 0, 8)
    expanded = jnp.repeat(jnp.repeat(levels_block, CX, axis=0), CY, axis=1)
    return (cell_draw < expanded).astype(jnp.int32)


def block_scale(stream_key, shape, shards, smallest, top_value):
    factor_of, own = 1.0, jax.random.fold_in(stream_key, 6)
    for axis_at, parts in shards:
        steps = jnp.exp(jax.random.uniform(jax.random.fold_in(own, axis_at), (parts,), jnp.float32, smallest / len(shards), top_value / len(shards)))
        factor_of = factor_of * jnp.repeat(steps, shape[axis_at] // parts).reshape([-1 if axis == axis_at else 1 for axis in range(len(shape))])
    return factor_of


def centred(key, extent, scale, bound, cuts=(), kind=jnp.bfloat16):
    gain = block_scale(key, extent, cuts, -0.22, 0.18) if cuts else 1.0
    array = jax.random.normal(key, extent, jnp.float32) * scale * gain
    return jnp.minimum(jnp.maximum(array, -bound), bound).astype(kind)


def setup_inputs(seed: int = 0) -> dict:
    streams_of = jax.random.split(jax.random.key(seed), 7)
    tracer = centred(streams_of[0], (2, TRACERS, LEVELS, NX, NY), 1.0, 6.0, ((0, 2), (3, 8), (4, 8)), jnp.float32)
    velocity = jnp.clip(jax.random.uniform(streams_of[1], (2, 2, LEVELS, NX, NY), jnp.float32, -0.2, 0.2) * block_scale(streams_of[1], (2, 2, LEVELS, NX, NY), ((0, 2), (3, 8), (4, 8)), -0.4, 0.0), -0.2, 0.2)
    mixing = jnp.clip(jnp.exp(math.log(0.12) - 1.3862944 * jax.random.uniform(streams_of[2], (2, LEVELS), jnp.float32) ** block_scale(streams_of[2], (2, LEVELS), ((0, 2),), -0.2, 0.2)), 0.03, 0.12)
    vertical_mixing = jnp.clip(jnp.exp(math.log(0.12) - 1.3862944 * jax.random.uniform(streams_of[3], (2, LEVELS), jnp.float32) ** block_scale(streams_of[3], (2, LEVELS), ((0, 2),), -0.2, 0.2)), 0.03, 0.12)
    transfer_coef = jnp.clip(jnp.exp(math.log(0.5) - 2.3025851 * jax.random.uniform(streams_of[4], (NX, NY), jnp.float32) ** block_scale(streams_of[4], (NX, NY), ((0, 8), (1, 8)), -0.2, 0.2)), 0.05, 0.5)
    land_mask = draw_land_mask(jax.random.fold_in(streams_of[6], 71), 0)
    return dict(tracer=tracer, velocity=velocity, mixing=mixing, vertical_mixing=vertical_mixing, transfer_coef=transfer_coef, land_mask=land_mask)


OCEAN_SHARE = 0.5


def advance(field, speeds, openness, horiz_mix, vert_mix):
    mix = horiz_mix[:, None, None]
    face_speed = 0.5 * (speeds[0, :, :-1, :] + speeds[0, :, 1:, :])
    face_open = openness[:-1, :] * openness[1:, :]
    west = field[..., :-1, :]
    east = field[..., 1:, :]
    flux_east = face_open * (face_speed * 0.5 * (west + east) - mix * (east - west))
    edge_row = jnp.zeros_like(flux_east[..., :1, :])
    padded_x = jnp.concatenate([edge_row, flux_east, edge_row], axis=-2)
    change_x = padded_x[..., :-1, :] - padded_x[..., 1:, :]
    side_speed = 0.5 * (speeds[1, :, :, :-1] + speeds[1, :, :, 1:])
    side_open = openness[:, :-1] * openness[:, 1:]
    south = field[..., :, :-1]
    north = field[..., :, 1:]
    flux_north = side_open * (side_speed * 0.5 * (south + north) - mix * (north - south))
    edge_col = jnp.zeros_like(flux_north[..., :, :1])
    padded_y = jnp.concatenate([edge_col, flux_north, edge_col], axis=-1)
    change_y = padded_y[..., :, :-1] - padded_y[..., :, 1:]
    lower = field[..., :-1, :, :]
    upper = field[..., 1:, :, :]
    flux_up = -vert_mix[:-1, None, None] * (upper - lower) * openness
    edge_level = jnp.zeros_like(flux_up[..., :1, :, :])
    padded_z = jnp.concatenate([edge_level, flux_up, edge_level], axis=-3)
    change_z = padded_z[..., :-1, :, :] - padded_z[..., 1:, :, :]
    return field + change_x + change_y + change_z


def reference(tracer, velocity, mixing, vertical_mixing, transfer_coef, land_mask):
    wet_cells = land_mask.astype(jnp.float32)
    atmosphere = tracer[0]
    ocean = tracer[1]
    surface_flux = transfer_coef * (ocean[:, 0] - atmosphere[:, LEVELS - 1]) * wet_cells
    atmosphere = atmosphere.at[:, LEVELS - 1].add(surface_flux)
    ocean = ocean.at[:, 0].add(-OCEAN_SHARE * surface_flux)
    all_open = jnp.ones_like(wet_cells)

    def run_atmosphere(column):
        for substep in range(SUBSTEPS):
            column = advance(column, velocity[0], all_open, mixing[0], vertical_mixing[0])
        return column

    def run_ocean(column):
        for substep in range(SUBSTEPS):
            column = advance(column, velocity[1], wet_cells, mixing[1], vertical_mixing[1])
        return column

    atmosphere = lax.map(run_atmosphere, atmosphere)
    ocean = lax.map(run_ocean, ocean)
    return jnp.stack([atmosphere, ocean])
```

```python
import jax
import jax.numpy as jnp
from jax import lax
from jax.experimental import pallas as pl
from jax.experimental.pallas import tpu as pltpu
from jax.sharding import PartitionSpec as P

SUBSTEPS = 4
OCEAN_SHARE = 0.5
T = 6
K = 8
CX, CY = 32, 128
R0, R1 = 12, 44
ROWS = 56
W = 4
SLOT = 20
MESH = pl.DeviceIdType.MESH


def kernel(tr, vel, mix, vmx, coef, mask, out, f0, f1, s0, s1, pw, pe, rw, re, uvs, cm, cs, res, msk, lsem, ssem, rsem):
    grp, lon, lat = lax.axis_index("grp"), lax.axis_index("lon"), lax.axis_index("lat")
    nlon, nlat = lax.axis_size("lon"), lax.axis_size("lat")
    ocean = grp == 1

    def level(k):
        return jnp.where(ocean, k, K - 1 - k)

    def exists(di, dj, sign=1):
        ok = None
        for pos, size, d in ((lon, nlon, di * sign), (lat, nlat, dj * sign)):
            if d:
                c = pos < size - 1 if d > 0 else pos > 0
                ok = c if ok is None else jnp.logical_and(ok, c)
        return ok

    def device(dg, di, dj):
        return {"grp": grp if dg == 0 else 1 - grp, "lon": lon + di, "lat": lat + dj}

    lo, hi, mid = slice(R0, R0 + W), slice(R1 - W, R1), slice(R0, R1)
    inlo, inhi = slice(R0 - W, R0), slice(R1, R1 + W)
    messages = []

    def message(where, src, dst):
        messages.append((where, src, dst))

    message((1, 0, 0), f0.at[0:T, 0, mid], f0.at[8, 2:8, mid])
    message((0, 1, 0), f0.at[0:8, :, hi], f0.at[0:8, :, inlo])
    message((0, -1, 0), f0.at[0:8, :, lo], f0.at[0:8, :, inhi])
    message((0, 1, 0), f0.at[8, 0:2, hi], f0.at[8, 0:2, inlo])
    message((0, -1, 0), f0.at[8, 0:2, lo], f0.at[8, 0:2, inhi])
    message((1, 1, 0), f0.at[0:T, 0, hi], f0.at[8, 2:8, inlo])
    message((1, -1, 0), f0.at[0:T, 0, lo], f0.at[8, 2:8, inhi])
    for dj, p, r in ((1, pw, rw), (-1, pe, re)):
        message((0, 0, dj), p.at[0:3, mid], r.at[0:3, mid])
        message((0, 1, dj), p.at[0:3, hi], r.at[0:3, inlo])
        message((0, -1, dj), p.at[0:3, lo], r.at[0:3, inhi])
        message((1, 0, dj), p.at[0, mid], r.at[3, mid])
        message((1, 1, dj), p.at[0, hi], r.at[3, inlo])
        message((1, -1, dj), p.at[0, lo], r.at[3, inhi])

    def remote(n):
        where, src, dst = messages[n]
        return pltpu.make_async_remote_copy(
            src_ref=src, dst_ref=dst, send_sem=ssem.at[n], recv_sem=rsem.at[n], device_id=device(*where), device_id_type=MESH
        )

    def guarded(ok, act):
        if ok is None:
            act()
        else:
            pl.when(ok)(act)

    loads = []
    for k in range(K):
        loads.append(pltpu.make_async_copy(tr.at[0, :, level(k)], f0.at[0:T, k, mid], lsem.at[k]))
        loads.append(pltpu.make_async_copy(vel.at[0, :, level(k)], f0.at[T : T + 2, k, mid], lsem.at[K + k]))
    loads.append(pltpu.make_async_copy(coef, f0.at[8, 1, mid], lsem.at[16]))
    loads.append(pltpu.make_async_copy(mask, msk, lsem.at[17]))

    def clear(ref, rows):
        shape = ref.shape[:-2] + (rows.stop - rows.start, CY)
        ref[..., rows, :] = jnp.zeros(shape, jnp.float32)

    @pl.when(lon == 0)
    def _():
        clear(f0, inlo), clear(rw, inlo), clear(re, inlo)

    @pl.when(lon == nlon - 1)
    def _():
        clear(f0, inhi), clear(rw, inhi), clear(re, inhi)

    @pl.when(lat == 0)
    def _():
        clear(rw, slice(R0 - W, R1 + W))

    @pl.when(lat == nlat - 1)
    def _():
        clear(re, slice(R0 - W, R1 + W))

    barrier = pltpu.get_barrier_semaphore()
    places = [(0, 0, 1), (0, 0, -1), (0, 1, 0), (0, -1, 0), (1, 0, 0)]
    places += [(0, a, b) for a in (1, -1) for b in (1, -1)]
    places += [(1, 1, 0), (1, -1, 0), (1, 0, 1), (1, 0, -1)]
    places += [(1, a, b) for a in (1, -1) for b in (1, -1)]
    met = 0
    for where in places:
        ok = exists(*where[1:])

        def greet(where=where):
            pl.semaphore_signal(barrier, inc=1, device_id=device(*where), device_id_type=MESH)

        guarded(ok, greet)
        met = met + (1 if ok is None else ok.astype(jnp.int32))

    for c in loads:
        c.start()
    for c in loads:
        c.wait()
    f0[8, 0, mid] = msk[...].astype(jnp.float32)

    lane = lax.broadcasted_iota(jnp.int32, (8, CY), 1)
    pos = lane % SLOT
    zero = jnp.zeros((8, CY), jnp.float32)

    def turn(x, shift):
        shift = shift % CY
        return x if shift == 0 else pltpu.roll(x, shift, 1)

    def between(a, b):
        return (lane >= a) & (lane < b)

    def pack(i, carry):
        rows = pl.ds(R0 + 8 * i, 8)
        for q in range(2):
            west, east = zero, zero
            for m in range(4):
                for t in range(T):
                    x = f0[t, 4 * q + m, rows]
                    at = t * SLOT + 4 * m
                    put = between(at, at + 4)
                    west = jnp.where(put, turn(x, at - (CY - W)), west)
                    east = jnp.where(put, turn(x, at), east)
            pw[q, rows], pe[q, rows] = west, east
        west, east = zero, zero
        for a in range(18):
            x = f0[6, a, rows] if a < 8 else f0[7, a - 8, rows] if a < 16 else f0[8, a - 16, rows]
            put = between(4 * a, 4 * a + 4)
            west = jnp.where(put, turn(x, 4 * a - (CY - W)), west)
            east = jnp.where(put, turn(x, 4 * a), east)
        pw[2, rows], pe[2, rows] = west, east
        return carry

    lax.fori_loop(0, 4, pack, 0)

    pl.semaphore_wait(barrier, met)
    for n, (where, _, _) in enumerate(messages):
        guarded(exists(*where[1:]), lambda n=n: remote(n).start())
    for n, (where, _, _) in enumerate(messages):
        guarded(exists(*where[1:], sign=-1), lambda n=n: remote(n).wait_recv())
        guarded(exists(*where[1:]), lambda n=n: remote(n).wait_send())

    def strips(i, carry):
        rows = pl.ds(pl.multiple_of(8 + 8 * i, 8), 8)
        far_w, far_e = pos < W, pos >= SLOT - W
        for k in range(K + 1):
            acc = zero
            for t in range(T):
                x = f0[t, k, rows] if k < K else f0[8, 2 + t, rows]
                at = t * SLOT
                acc = jnp.where(between(at + 4, at + 10), turn(x, at + 4), acc)
                acc = jnp.where(between(at + 10, at + 16), turn(x, at + 10 - 122), acc)
            q, m = (k // 4, k % 4) if k < K else (3, 0)
            acc = jnp.where(far_w, turn(rw[q, rows], -4 * m), acc)
            acc = jnp.where(far_e, turn(re[q, rows], 16 - 4 * m), acc)
            s0[k, rows] = jnp.where(lane < T * SLOT, acc, 0.0)
        for a in range(18):
            x = f0[6, a, rows] if a < 8 else f0[7, a - 8, rows] if a < 16 else f0[8, a - 16, rows]
            acc = jnp.where(between(4, 10), turn(x, 4), zero)
            acc = jnp.where(between(10, 16), turn(x, 10 - 122), acc)
            acc = jnp.where(between(0, 4), turn(rw[2, rows], -4 * a), acc)
            acc = jnp.where(between(16, 20), turn(re[2, rows], 16 - 4 * a), acc)
            two = acc + turn(acc, 20)
            uvs[a, rows] = two + turn(two, 40) + turn(two, 80)
        return carry

    lax.fori_loop(0, 5, strips, 0)

    sub = lax.broadcasted_iota(jnp.int32, (8, CY), 0)
    beyond_w = (pos < W) & (lat == 0)
    beyond_e = (pos >= SLOT - W) & (lat == nlat - 1)

    def opening(i, carry):
        rows = pl.ds(pl.multiple_of(8 + 8 * i, 8), 8)
        row = 8 + 8 * i + sub
        shut = ((row < R0) & (lon == 0)) | ((row >= R1) & (lon == nlon - 1))
        wet = f0[8, 0, rows]
        cm[6, 0, rows] = jnp.where(shut, 0.0, jnp.where(ocean, wet, 1.0))
        wet = uvs[16, rows]
        cs[6, 0, rows] = jnp.where(shut | beyond_w | beyond_e, 0.0, jnp.where(ocean, wet, 1.0))
        share = jnp.where(ocean, OCEAN_SHARE, 1.0)
        gain = share * f0[8, 1, rows] * f0[8, 0, rows]
        for t in range(T):
            x = f0[t, 0, rows]
            f0[t, 0, rows] = x + gain * (f0[8, 2 + t, rows] - x)
        x = s0[0, rows]
        s0[0, rows] = x + share * uvs[17, rows] * uvs[16, rows] * (s0[8, rows] - x)
        return carry

    lax.fori_loop(0, 5, opening, 0)

    def coefficients(c, u, v):
        def some_rows(i, carry):
            o = 8 + 8 * i
            rows = pl.ds(pl.multiple_of(o, 8), 8)
            before, after = pl.ds(o - 1, 8), pl.ds(o + 1, 8)
            w = c[6, 0, rows]
            wb, wa = w * c[6, 0, before], w * c[6, 0, after]
            ws, wn = w * turn(w, 1), w * turn(w, -1)
            below = None
            for k in range(K):
                h = mix[0, level(k)]
                uk, vk = u(k, rows), v(k, rows)
                sb, sa = 0.25 * (u(k, before) + uk), 0.25 * (u(k, after) + uk)
                ss, sn = 0.25 * (turn(vk, 1) + vk), 0.25 * (turn(vk, -1) + vk)
                c[1, k, rows] = wb * (sb + h)
                c[2, k, rows] = wa * (h - sa)
                c[3, k, rows] = ws * (ss + h)
                c[4, k, rows] = wn * (h - sn)
                own = 1.0 + (wb * (sb - h) - wa * (sa + h)) + (ws * (ss - h) - wn * (sn + h))
                if k > 0:
                    own = own - below
                if k < K - 1:
                    below = w * vmx[0, jnp.where(ocean, k, K - 2 - k)]
                    c[5, k, rows] = below
                    own = own - below
                c[0, k, rows] = own
            return carry

        lax.fori_loop(0, 5, some_rows, 0)

    coefficients(cm, lambda k, rows: f0[6, k, rows], lambda k, rows: f0[7, k, rows])
    coefficients(cs, lambda k, rows: uvs[k, rows], lambda k, rows: uvs[8 + k, rows])

    def substep(load, c, n, o, rows, store):
        before, after = pl.ds(o - 1, 8), pl.ds(o + 1, 8)
        own = [load(t, 0, rows) for t in range(n)]
        last = [None] * n
        below = None
        for k in range(K):
            co, cb, ca, cso, cno = (c[j, k, rows] for j in range(5))
            up = c[5, k, rows] if k < K - 1 else None
            for t in range(n):
                x = own[t]
                y = co * x + cb * load(t, k, before) + ca * load(t, k, after)
                y = y + cso * turn(x, 1) + cno * turn(x, -1)
                if k > 0:
                    y = y + below * last[t]
                if k < K - 1:
                    own[t] = load(t, k + 1, rows)
                    y = y + up * own[t]
                last[t] = x
                store(t, k, y)
            below = up

    def from_strip(k, rows, s):
        x = s[k, rows]
        return jnp.where((pos == 2) | (pos == 3), turn(x, -12), x)

    edge = (lane < 2) | (lane >= CY - 2)

    def advance(src, ssrc, dst, sdst, refresh):
        def some_rows(i, carry):
            o = 8 + 8 * i
            rows = pl.ds(pl.multiple_of(o, 8), 8)

            def keep(t, k, y):
                sdst[k, rows] = y

            substep(lambda t, k, r: ssrc[k, r], cs, 1, o, rows, keep)

            def put(t, k, y):
                if refresh:
                    if t == 0:
                        put.x = from_strip(k, rows, sdst)
                    y = jnp.where(edge, turn(put.x, 126 - (t * SLOT + 2)), y)
                dst[t, k, rows] = y

            substep(lambda t, k, r: src[t, k, r], cm, T, o, rows, put)
            return carry

        lax.fori_loop(0, 5, some_rows, 0)

    advance(f0, s0, f1, s1, False)
    advance(f1, s1, f0, s0, True)
    advance(f0, s0, f1, s1, False)

    def last_rows(i, carry):
        o = R0 + 8 * i
        rows = pl.ds(o, 8)

        def keep(t, k, y):
            s0[k, rows] = y

        substep(lambda t, k, r: s1[k, r], cs, 1, o, rows, keep)
        orows = pl.ds(pl.multiple_of(8 * i, 8), 8)

        def put(t, k, y):
            if t == 0:
                put.x = from_strip(k, rows, s0)
            res[t, k, orows] = jnp.where(edge, turn(put.x, 126 - (t * SLOT + 2)), y)

        substep(lambda t, k, r: f1[t, k, r], cm, T, o, rows, put)
        return carry

    lax.fori_loop(0, 4, last_rows, 0)

    stores = [pltpu.make_async_copy(res.at[:, k], out.at[0, :, level(k)], lsem.at[k]) for k in range(K)]
    for c in stores:
        c.start()
    for c in stores:
        c.wait()


N_MESSAGES = 19


def body(tracer, velocity, mixing, vertical_mixing, transfer_coef, land_mask):
    f32 = jnp.float32
    anywhere = pl.BlockSpec(memory_space=pl.ANY)
    scalars = pl.BlockSpec(memory_space=pltpu.SMEM)
    return pl.pallas_call(
        kernel,
        out_shape=jax.ShapeDtypeStruct(tracer.shape, f32),
        in_specs=[anywhere, anywhere, scalars, scalars, anywhere, anywhere],
        out_specs=anywhere,
        scratch_shapes=[
            pltpu.VMEM((9, K, ROWS, CY), f32),
            pltpu.VMEM((T, K, ROWS, CY), f32),
            pltpu.VMEM((K + 1, ROWS, CY), f32),
            pltpu.VMEM((K, ROWS, CY), f32),
            pltpu.VMEM((3, ROWS, CY), f32),
            pltpu.VMEM((3, ROWS, CY), f32),
            pltpu.VMEM((4, ROWS, CY), f32),
            pltpu.VMEM((4, ROWS, CY), f32),
            pltpu.VMEM((18, ROWS, CY), f32),
            pltpu.VMEM((7, K, ROWS, CY), f32),
            pltpu.VMEM((7, K, ROWS, CY), f32),
            pltpu.VMEM((T, K, CX, CY), f32),
            pltpu.VMEM((CX, CY), jnp.int32),
            pltpu.SemaphoreType.DMA((18,)),
            pltpu.SemaphoreType.DMA((N_MESSAGES,)),
            pltpu.SemaphoreType.DMA((N_MESSAGES,)),
        ],
        compiler_params=pltpu.CompilerParams(collective_id=0, has_side_effects=True),
        name="interval",
    )(tracer, velocity, mixing, vertical_mixing, transfer_coef, land_mask)


def solution(mesh):
    return jax.shard_map(
        body,
        mesh=mesh,
        in_specs=(
            P("grp", None, None, "lon", "lat"),
            P("grp", None, None, "lon", "lat"),
            P("grp", None),
            P("grp", None),
            P("lon", "lat"),
            P("lon", "lat"),
        ),
        out_specs=P("grp", None, None, "lon", "lat"),
        check_vma=False,
    )
```

```python
import jax
import jax.numpy as jnp
from jax import lax
from jax.experimental import pallas as pl
from jax.experimental.pallas import tpu as pltpu
from jax.sharding import PartitionSpec as P

SUBSTEPS = 4
OCEAN_SHARE = 0.5
T = 6
K = 8
CX, CY = 32, 128
R0, R1 = 12, 44
ROWS = 56
W = 4
SLOT = 20
OWN = 8
SURFACE, U, V, WET, TRANSFER, PLANES = T, T + T * K, T + T * K + K, 70, 71, 72
FIELDS = 2 * K + 2
MESH = pl.DeviceIdType.MESH


def kernel(tr, vel, mix, vmx, coef, mask, out, f0, f1, sw0, sw1, se0, se1, pw, pe, rw, re, uw, ue, c, msk, lsem, ssem, rsem):
    grp, lon, lat = lax.axis_index("grp"), lax.axis_index("lon"), lax.axis_index("lat")
    nlon, nlat = lax.axis_size("lon"), lax.axis_size("lat")
    ocean = grp == 1

    def exists(di, dj, sign=1):
        ok = None
        for pos, size, d in ((lon, nlon, di * sign), (lat, nlat, dj * sign)):
            if d:
                one = pos < size - 1 if d > 0 else pos > 0
                ok = one if ok is None else jnp.logical_and(ok, one)
        return ok

    def device(dg, di, dj):
        return {"grp": grp if dg == 0 else 1 - grp, "lon": lon + di, "lat": lat + dj}

    def guarded(ok, act):
        if ok is None:
            act()
        else:
            pl.when(ok)(act)

    barrier = pltpu.get_barrier_semaphore()
    places = [(1, a, b) for a in (1, -1) for b in (1, -1)]
    places += [(0, a, b) for a in (1, -1) for b in (1, -1)]
    places += [(1, 1, 0), (1, -1, 0), (1, 0, 1), (1, 0, -1)]
    places += [(1, 0, 0), (0, 0, 1), (0, 0, -1), (0, 1, 0), (0, -1, 0)]
    for where in places:

        def greet(where=where):
            pl.semaphore_signal(barrier, inc=1, device_id=device(*where), device_id_type=MESH)

        guarded(exists(*where[1:]), greet)
    beside = (lon > 0).astype(jnp.int32) + (lon < nlon - 1).astype(jnp.int32)
    along = (lat > 0).astype(jnp.int32) + (lat < nlat - 1).astype(jnp.int32)
    met = 2 * (1 + beside) * (1 + along) - 1

    def level(k):
        return jnp.where(ocean, k, K - 1 - k)

    lo, hi, mid = pl.ds(R0, W), pl.ds(R1 - W, W), pl.ds(R0, CX)
    inlo, inhi = pl.ds(R0 - W, W), pl.ds(R1, W)

    def fetch(k, carry):
        pltpu.make_async_copy(tr.at[0, :, level(k)], f0.at[pl.ds(SURFACE + T * k, T), mid], lsem.at[0]).start()
        pltpu.make_async_copy(vel.at[0, 0, level(k)], f0.at[U + k, mid], lsem.at[0]).start()
        pltpu.make_async_copy(vel.at[0, 1, level(k)], f0.at[V + k, mid], lsem.at[0]).start()
        return carry

    pltpu.make_async_copy(mask, msk, lsem.at[1]).start()
    pltpu.make_async_copy(coef, f0.at[TRANSFER, mid], lsem.at[0]).start()
    lax.fori_loop(0, K, fetch, 0)

    def clear(ref, n, first, count):
        def one(j, carry):
            ref[j, pl.ds(first, count)] = jnp.zeros((count, CY), jnp.float32)
            return carry

        lax.fori_loop(0, n, one, 0)

    @pl.when(lon == 0)
    def _():
        clear(f0, PLANES, R0 - W, W), clear(rw, 4, R0 - W, W), clear(re, 4, R0 - W, W)

    @pl.when(lon == nlon - 1)
    def _():
        clear(f0, PLANES, R1, W), clear(rw, 4, R1, W), clear(re, 4, R1, W)

    @pl.when(lat == 0)
    def _():
        clear(rw, 4, R0 - W, CX + 2 * W)

    @pl.when(lat == nlat - 1)
    def _():
        clear(re, 4, R0 - W, CX + 2 * W)

    lane = lax.broadcasted_iota(jnp.int32, (8, CY), 1)
    sub = lax.broadcasted_iota(jnp.int32, (8, CY), 0)
    zero = jnp.zeros((8, CY), jnp.float32)
    pos = lane % SLOT
    ahead = (lane + W) % CY
    epos = ahead % SLOT
    far_w = (pos < W) & (lane < T * SLOT)
    far_e = (epos >= OWN) & (epos < OWN + W) & (ahead < T * SLOT)

    def turn(x, shift):
        shift = shift % CY
        return x if shift == 0 else pltpu.roll(x, shift, 1)

    def between(x, a, n):
        return (x >= a) & (x < a + n)

    pltpu.make_async_copy(mask, msk, lsem.at[1]).wait()
    total = pl.ds(0, T * K + 2 * K + 1)
    pltpu.make_async_copy(f0.at[total, mid], f0.at[total, mid], lsem.at[0]).wait()
    f0[WET, mid] = msk[...].astype(jnp.float32)

    def pack(i, carry):
        rows = pl.ds(R0 + 8 * i, 8)
        for q in range(2):
            west, east = zero, zero
            for m in range(4):
                for t in range(T):
                    x = f0[SURFACE + T * (4 * q + m) + t, rows]
                    at = t * SLOT + 4 * m
                    put = between(lane, at, W)
                    west = jnp.where(put, turn(x, at - (CY - W)), west)
                    east = jnp.where(put, turn(x, at), east)
            pw[q, rows], pe[q, rows] = west, east
        west, east = zero, zero
        for a in range(FIELDS):
            x = f0[U + a, rows]
            put = between(lane, 4 * a, W)
            west = jnp.where(put, turn(x, 4 * a - (CY - W)), west)
            east = jnp.where(put, turn(x, 4 * a), east)
        pw[2, rows], pe[2, rows] = west, east
        return carry

    lax.fori_loop(0, CX // 8, pack, 0)

    near, far = [], []
    for dj, p, r in ((1, pw, rw), (-1, pe, re)):
        packs = pl.ds(0, 3)
        near.append(((0, 0, dj), p.at[packs, mid], r.at[packs, mid]))
        near.append(((0, 1, dj), p.at[packs, hi], r.at[packs, inlo]))
        near.append(((0, -1, dj), p.at[packs, lo], r.at[packs, inhi]))
        far.append(((1, 0, dj), p.at[0, mid], r.at[3, mid]))
        far.append(((1, 1, dj), p.at[0, hi], r.at[3, inlo]))
        far.append(((1, -1, dj), p.at[0, lo], r.at[3, inhi]))
    block = pl.ds(SURFACE, PLANES - SURFACE)
    near.append(((0, 1, 0), f0.at[block, hi], f0.at[block, inlo]))
    near.append(((0, -1, 0), f0.at[block, lo], f0.at[block, inhi]))
    surface, other = pl.ds(SURFACE, T), pl.ds(0, T)
    far.append(((1, 1, 0), f0.at[surface, hi], f0.at[other, inlo]))
    far.append(((1, -1, 0), f0.at[surface, lo], f0.at[other, inhi]))
    far.append(((1, 0, 0), f0.at[surface, mid], f0.at[other, mid]))
    messages = near + far

    def remote(n):
        where, src, dst = messages[n]
        return pltpu.make_async_remote_copy(
            src_ref=src, dst_ref=dst, send_sem=ssem.at[n], recv_sem=rsem.at[n], device_id=device(*where), device_id_type=MESH
        )

    def arrived(n):
        guarded(exists(*messages[n][0][1:], sign=-1), lambda: remote(n).wait_recv())

    def sent(n):
        guarded(exists(*messages[n][0][1:]), lambda: remote(n).wait_send())

    pl.semaphore_wait(barrier, met)
    for n in range(len(messages)):
        guarded(exists(*messages[n][0][1:]), lambda n=n: remote(n).start())

    def pads(i, carry):
        rows = pl.ds(pl.multiple_of(8 + 8 * i, 8), 8)
        for t in range(T):
            f1[t, rows] = zero
            f1[T + T * K + t, rows] = zero
        for s in (sw0, se0, sw1, se1):
            s[0, rows] = zero
            s[K + 1, rows] = zero
        for j in range(3):
            c[j, 5, 0, rows] = zero
            c[j, 5, K, rows] = zero
        return carry

    lax.fori_loop(0, 5, pads, 0)

    def coefficients(side, o, rows, u, v):
        before, after = pl.ds(o - 1, 8), pl.ds(o + 1, 8)
        w = opening(side, o, rows)
        wb, wa = w * opening(side, o - 1, before), w * opening(side, o + 1, after)
        ws, wn = w * turn(w, 1), w * turn(w, -1)
        above = None
        for k in range(K):
            h = mix[0, level(k)]
            uk, vk = u(k, rows), v(k, rows)
            sb, sa = 0.25 * (u(k, before) + uk), 0.25 * (u(k, after) + uk)
            ss, sn = 0.25 * (turn(vk, 1) + vk), 0.25 * (turn(vk, -1) + vk)
            c[side, 1, k, rows] = wb * (sb + h)
            c[side, 2, k, rows] = wa * (h - sa)
            c[side, 3, k, rows] = ws * (ss + h)
            c[side, 4, k, rows] = wn * (h - sn)
            own = 1.0 + (wb * (sb - h) - wa * (sa + h)) + (ws * (ss - h) - wn * (sn + h))
            if k > 0:
                own = own - above
            if k < K - 1:
                above = w * vmx[0, jnp.where(ocean, k, K - 2 - k)]
                c[side, 5, k + 1, rows] = above
                own = own - above
            c[side, 0, k, rows] = own

    def opening(side, o, rows):
        row = o + sub
        shut = ((row < R0) & (lon == 0)) | ((row >= R1) & (lon == nlon - 1))
        if side == 1:
            shut = shut | (far_w & (lat == 0))
        if side == 2:
            shut = shut | (far_e & (lat == nlat - 1))
        wet = f0[WET, rows] if side == 0 else uw[2 * K, rows] if side == 1 else ue[2 * K, rows]
        return jnp.where(shut, 0.0, jnp.where(ocean, wet, 1.0))

    def own_strips(first, rows):
        west, east = zero, zero
        for t in range(T):
            x = f0[first + t, rows]
            at = t * SLOT
            west = jnp.where(between(lane, at + W, OWN), turn(x, at + W), west)
            east = jnp.where(between(ahead, at, OWN), turn(x, at - W - (CY - OWN)), east)
        return west, east

    def repeat(x):
        two = x + turn(x, SLOT)
        return two + turn(two, 2 * SLOT) + turn(two, 4 * SLOT)

    def inner(i, carry):
        @pl.when(i == 3)
        def _():
            for n in range(len(near)):
                arrived(n)

        o = pl.multiple_of(jnp.where(i < 3, 16 + 8 * i, 8 + 32 * (i - 3)), 8)
        rows = pl.ds(o, 8)
        for k in range(K):
            sw0[k + 1, rows], se0[k + 1, rows] = own_strips(SURFACE + T * k, rows)
        for a in range(FIELDS):
            x = f0[U + a, rows]
            uw[a, rows] = repeat(jnp.where(between(lane, W, OWN), turn(x, W), zero))
            ue[a, rows] = repeat(jnp.where(between(ahead, 0, OWN), turn(x, -W - (CY - OWN)), zero))
        coefficients(0, o, rows, lambda k, r: f0[U + k, r], lambda k, r: f0[V + k, r])
        return carry

    lax.fori_loop(0, 5, inner, 0)

    def outer(i, carry):
        rows = pl.ds(pl.multiple_of(8 + 8 * i, 8), 8)
        for k in range(K):
            q, m = k // 4, k % 4
            sw0[k + 1, rows] = jnp.where(far_w, turn(rw[q, rows], -4 * m), sw0[k + 1, rows])
            se0[k + 1, rows] = jnp.where(far_e, turn(re[q, rows], W - 4 * m), se0[k + 1, rows])
        for a in range(FIELDS):
            uw[a, rows] = uw[a, rows] + repeat(jnp.where(between(lane, 0, W), turn(rw[2, rows], -4 * a), zero))
            ue[a, rows] = ue[a, rows] + repeat(jnp.where(between(ahead, OWN, W), turn(re[2, rows], W - 4 * a), zero))
        return carry

    lax.fori_loop(0, 5, outer, 0)

    def edges(i, carry):
        o = 8 + 8 * i
        rows = pl.ds(pl.multiple_of(o, 8), 8)
        coefficients(1, o, rows, lambda k, r: uw[k, r], lambda k, r: uw[K + k, r])
        coefficients(2, o, rows, lambda k, r: ue[k, r], lambda k, r: ue[K + k, r])
        return carry

    lax.fori_loop(0, 5, edges, 0)
    for n in range(len(near)):
        sent(n)

    def stencil(side, src, n, k, o):
        rows, before, after = pl.ds(o, 8), pl.ds(o - 1, 8), pl.ds(o + 1, 8)
        co, cb, ca, cs, cn = (c[side, j, k, rows] for j in range(5))
        above, below = c[side, 5, k, rows], c[side, 5, k + 1, rows]
        for t in range(n):
            p = (k + 1) * n + t
            x = src[p, rows]
            y = co * x + cb * src[p, before] + ca * src[p, after]
            y = y + (cs * turn(x, 1) + cn * turn(x, -1))
            yield t, y + (above * src[p - n, rows] + below * src[p + n, rows])

    def substep(src, dst, first, last):
        def one(k, carry):
            for i in range(5):
                o = 8 + 8 * i
                for side, n in ((1, 1), (2, 1), (0, T)):
                    for t, y in stencil(side, src[side], n, k, o):
                        dst[side][(k + 1) * n + t, pl.ds(o, 8)] = y
            return carry

        lax.fori_loop(first, last, one, 0)

    def finish(src, first, last):
        stale = (lane < W) | (lane >= CY - W)

        def one(k, carry):
            for i in range(CX // 8):
                o = R0 + 8 * i
                ((_, west),) = stencil(1, src[1], 1, k, o)
                ((_, east),) = stencil(2, src[2], 1, k, o)
                fresh = jnp.where(pos < W, east, west)
                for t, y in stencil(0, src[0], T, k, o):
                    out[0, t, level(k), pl.ds(8 * i, 8)] = jnp.where(stale, turn(fresh, CY - W - t * SLOT), y)
            return carry

        lax.fori_loop(first, last, one, 0)

    share = jnp.where(ocean, OCEAN_SHARE, 1.0)

    def exchange(i, carry):
        rows = pl.ds(pl.multiple_of(8 + 8 * i, 8), 8)
        gain = share * f0[TRANSFER, rows] * f0[WET, rows]
        for t in range(T):
            x = f0[SURFACE + t, rows]
            f0[SURFACE + t, rows] = x + gain * (f0[t, rows] - x)
        west, east = own_strips(0, rows)
        west = jnp.where(far_w, rw[3, rows], west)
        east = jnp.where(far_e, turn(re[3, rows], W), east)
        for s, fields, theirs in ((sw0, uw, west), (se0, ue, east)):
            x = s[1, rows]
            s[1, rows] = x + share * fields[2 * K + 1, rows] * fields[2 * K, rows] * (theirs - x)
        return carry

    even, odd = (f0, sw0, se0), (f1, sw1, se1)

    def phase(late, carry):
        @pl.when(late == 1)
        def _():
            for n in range(len(near), len(messages)):
                sent(n)
            for n in range(len(near), len(messages)):
                arrived(n)
            lax.fori_loop(0, 5, exchange, 0)

        def bounds(s):
            return (s + 1) * (1 - late), K - late * (K - 1 - s)

        def two(j, carry):
            substep(even, odd, *bounds(1 + 2 * j))
            first, last = bounds(2 + 2 * j)
            substep(odd, even, first, first + (last - first) * (1 - j))
            finish(odd, first, first + (last - first) * j)
            return carry

        return lax.fori_loop(0, SUBSTEPS // 2, two, carry)

    lax.fori_loop(0, 2, phase, 0)


N_MESSAGES = 17


def body(tracer, velocity, mixing, vertical_mixing, transfer_coef, land_mask):
    f32 = jnp.float32
    anywhere = pl.BlockSpec(memory_space=pl.ANY)
    scalars = pl.BlockSpec(memory_space=pltpu.SMEM)

    def planes(*n):
        return pltpu.VMEM((*n, ROWS, CY), f32)

    return pl.pallas_call(
        kernel,
        out_shape=pltpu.VMEM(tracer.shape, f32),
        in_specs=[anywhere, anywhere, scalars, scalars, anywhere, anywhere],
        out_specs=pl.BlockSpec(memory_space=pltpu.VMEM),
        scratch_shapes=[
            planes(PLANES),
            planes(T * (K + 2)),
            *[planes(K + 2)] * 4,
            *[planes(3)] * 2,
            *[planes(4)] * 2,
            *[planes(FIELDS)] * 2,
            planes(3, 6, K + 1),
            pltpu.VMEM((CX, CY), jnp.int32),
            pltpu.SemaphoreType.DMA((2,)),
            pltpu.SemaphoreType.DMA((N_MESSAGES,)),
            pltpu.SemaphoreType.DMA((N_MESSAGES,)),
        ],
        compiler_params=pltpu.CompilerParams(collective_id=0, has_side_effects=True),
        name="interval",
    )(tracer, velocity, mixing, vertical_mixing, transfer_coef, land_mask)


def solution(mesh):
    return jax.shard_map(
        body,
        mesh=mesh,
        in_specs=(
            P("grp", None, None, "lon", "lat"),
            P("grp", None, None, "lon", "lat"),
            P("grp", None),
            P("grp", None),
            P("lon", "lat"),
            P("lon", "lat"),
        ),
        out_specs=P("grp", None, None, "lon", "lat"),
        check_vma=False,
    )
```

```python
import jax
import jax.numpy as jnp
from jax import lax
from jax.experimental import pallas as pl
from jax.experimental.pallas import tpu as pltpu
from jax.sharding import PartitionSpec as P

SUBSTEPS = 4
OCEAN_SHARE = 0.5
T = 6
K = 8
CX, CY = 32, 128
R0, R1 = 12, 44
ROWS = 56
W = 4
SLOT = 16
OWN = 8
SURFACE, U, V, WET, TRANSFER, PLANES = T, T + T * K, T + T * K + K, 70, 71, 72
MESH = pl.DeviceIdType.MESH


def kernel(tr, vel, mix, vmx, coef, mask, out, f0, f1, f2, f3, sw0, sw1, se0, se1, pw, pe, rw, re, uw, ue, c, cw, ce, hs, msk, lsem, ssem, rsem):
    grp, lon, lat = lax.axis_index("grp"), lax.axis_index("lon"), lax.axis_index("lat")
    nlon, nlat = lax.axis_size("lon"), lax.axis_size("lat")
    ocean = grp == 1

    def exists(di, dj, sign=1):
        ok = None
        for pos, size, d in ((lon, nlon, di * sign), (lat, nlat, dj * sign)):
            if d:
                one = pos < size - 1 if d > 0 else pos > 0
                ok = one if ok is None else jnp.logical_and(ok, one)
        return ok

    def device(dg, di, dj):
        return {"grp": grp if dg == 0 else 1 - grp, "lon": lon + di, "lat": lat + dj}

    def guarded(ok, act):
        if ok is None:
            act()
        else:
            pl.when(ok)(act)

    barrier = pltpu.get_barrier_semaphore()
    places = [(1, a, b) for a in (1, -1) for b in (1, -1)]
    places += [(0, a, b) for a in (1, -1) for b in (1, -1)]
    places += [(1, 1, 0), (1, -1, 0), (1, 0, 1), (1, 0, -1)]
    places += [(1, 0, 0), (0, 0, 1), (0, 0, -1), (0, 1, 0), (0, -1, 0)]
    for where in places:

        def greet(where=where):
            pl.semaphore_signal(barrier, inc=1, device_id=device(*where), device_id_type=MESH)

        guarded(exists(*where[1:]), greet)
    beside = (lon > 0).astype(jnp.int32) + (lon < nlon - 1).astype(jnp.int32)
    along = (lat > 0).astype(jnp.int32) + (lat < nlat - 1).astype(jnp.int32)
    met = 2 * (1 + beside) * (1 + along) - 1

    def level(k):
        return jnp.where(ocean, k, K - 1 - k)

    lo, hi, mid = pl.ds(R0, W), pl.ds(R1 - W, W), pl.ds(R0, CX)
    inlo, inhi = pl.ds(R0 - W, W), pl.ds(R1, W)

    def fetch(k, carry):
        pltpu.make_async_copy(tr.at[0, :, level(k)], f0.at[pl.ds(SURFACE + T * k, T), mid], lsem.at[0]).start()
        pltpu.make_async_copy(vel.at[0, 0, level(k)], f0.at[U + k, mid], lsem.at[0]).start()
        pltpu.make_async_copy(vel.at[0, 1, level(k)], f0.at[V + k, mid], lsem.at[0]).start()
        return carry

    pltpu.make_async_copy(mask, msk, lsem.at[1]).start()
    pltpu.make_async_copy(coef, f0.at[TRANSFER, mid], lsem.at[0]).start()
    lax.fori_loop(0, K, fetch, 0)

    def clear(ref, n, first, count):
        def one(j, carry):
            ref[j, pl.ds(first, count)] = jnp.zeros((count, CY), jnp.float32)
            return carry

        lax.fori_loop(0, n, one, 0)

    @pl.when(lon == 0)
    def _():
        clear(f0, PLANES, R0 - W, W), clear(rw, 4, R0 - W, W), clear(re, 4, R0 - W, W)

    @pl.when(lon == nlon - 1)
    def _():
        clear(f0, PLANES, R1, W), clear(rw, 4, R1, W), clear(re, 4, R1, W)

    @pl.when(lat == 0)
    def _():
        clear(rw, 4, R0 - W, CX + 2 * W)

    @pl.when(lat == nlat - 1)
    def _():
        clear(re, 4, R0 - W, CX + 2 * W)

    lane = lax.broadcasted_iota(jnp.int32, (8, CY), 1)
    sub = lax.broadcasted_iota(jnp.int32, (8, CY), 0)
    zero = jnp.zeros((8, CY), jnp.float32)
    ahead = (lane + W) % CY
    slot = ahead // SLOT
    part = (lane % SLOT) // W
    far_w, far_e = part == 0, part == 1
    def turn(x, shift):
        shift = shift % CY
        return x if shift == 0 else pltpu.roll(x, shift, 1)

    def between(x, a, n):
        return (x >= a) & (x < a + n)

    pltpu.make_async_copy(mask, msk, lsem.at[1]).wait()
    total = pl.ds(0, T * K + 2 * K + 1)
    pltpu.make_async_copy(f0.at[total, mid], f0.at[total, mid], lsem.at[0]).wait()
    f0[WET, mid] = msk[...].astype(jnp.float32)

    def own_edges(ch, rows):
        acc = zero
        for k in range(K):
            x = f0[SURFACE + T * k + ch if ch < T else U + K * (ch - T) + k, rows]
            acc = jnp.where(slot == k, turn(x, SLOT * k + W), acc)
        return acc

    def pack(i, carry):
        rows = pl.ds(R0 + 8 * i, 8)
        west, east = [zero, zero, zero], [zero, zero, zero]
        for ch in range(T + 2):
            x, q, m = own_edges(ch, rows), ch // 4, ch % 4
            west[q] = jnp.where(part == m, turn(x, W * m), west[q])
            east[q] = jnp.where(part == m, turn(x, W * m - W), east[q])
            if ch < T:
                put = between(lane, W * (ch + 2), W)
                west[2] = jnp.where(put, turn(x, W * (ch + 2)), west[2])
                east[2] = jnp.where(put, turn(x, W * (ch + 1)), east[2])
        for j, plane in enumerate((WET, TRANSFER)):
            x, put = f0[plane, rows], between(lane, W * j, W)
            west[2] = jnp.where(put, turn(x, W * (j + 1)), west[2])
            east[2] = jnp.where(put, turn(x, W * j), east[2])
        for q in range(3):
            pw[q, rows], pe[q, rows] = west[q], east[q]
        return carry

    lax.fori_loop(0, CX // 8, pack, 0)

    near, far = [], []
    for dj, p, r in ((1, pw, rw), (-1, pe, re)):
        packs = pl.ds(0, 3)
        near.append(((0, 0, dj), p.at[packs, mid], r.at[packs, mid]))
        near.append(((0, 1, dj), p.at[packs, hi], r.at[packs, inlo]))
        near.append(((0, -1, dj), p.at[packs, lo], r.at[packs, inhi]))
        far.append(((1, 0, dj), p.at[2, mid], r.at[3, mid]))
        far.append(((1, 1, dj), p.at[2, hi], r.at[3, inlo]))
        far.append(((1, -1, dj), p.at[2, lo], r.at[3, inhi]))
    block = pl.ds(SURFACE, PLANES - SURFACE)
    near.append(((0, 1, 0), f0.at[block, hi], f0.at[block, inlo]))
    near.append(((0, -1, 0), f0.at[block, lo], f0.at[block, inhi]))
    surface, other = pl.ds(SURFACE, T), pl.ds(0, T)
    far.append(((1, 1, 0), f0.at[surface, hi], f0.at[other, inlo]))
    far.append(((1, -1, 0), f0.at[surface, lo], f0.at[other, inhi]))
    far.append(((1, 0, 0), f0.at[surface, mid], f0.at[other, mid]))
    messages = near + far

    def remote(n):
        where, src, dst = messages[n]
        return pltpu.make_async_remote_copy(
            src_ref=src, dst_ref=dst, send_sem=ssem.at[n], recv_sem=rsem.at[n], device_id=device(*where), device_id_type=MESH
        )

    def arrived(n):
        guarded(exists(*messages[n][0][1:], sign=-1), lambda: remote(n).wait_recv())

    def sent(n):
        guarded(exists(*messages[n][0][1:]), lambda: remote(n).wait_send())

    pl.semaphore_wait(barrier, met)
    for n in range(len(messages)):
        guarded(exists(*messages[n][0][1:]), lambda n=n: remote(n).start())

    def pads(i, carry):
        rows = pl.ds(pl.multiple_of(8 + 8 * i, 8), 8)
        for f in (f1, f2, f3):
            for t in range(T):
                f[t, rows] = zero
                f[T + T * K + t, rows] = zero
        c[5, 0, rows] = zero
        c[5, K, rows] = zero
        return carry

    lax.fori_loop(0, 5, pads, 0)

    def number(k):
        return vmx[0, jnp.where(ocean, k, K - 2 - k)]

    for side, its in enumerate((lane // SLOT, slot)):
        h, up, down = zero, zero, zero
        for k in range(K):
            h = jnp.where(its == k, mix[0, level(k)], h)
            if k > 0:
                up = jnp.where(its == k, number(k - 1), up)
            if k < K - 1:
                down = jnp.where(its == k, number(k), down)
        hs[side, 0], hs[side, 1], hs[side, 2] = h, up, down

    def faces(h, w, wb, wa, u, ub, ua, v):
        wb, wa = w * wb, w * wa
        ws, wn = w * turn(w, 1), w * turn(w, -1)
        sb, sa = 0.25 * (ub + u), 0.25 * (ua + u)
        ss, sn = 0.25 * (turn(v, 1) + v), 0.25 * (turn(v, -1) + v)
        own = 1.0 + (wb * (sb - h) - wa * (sa + h)) + (ws * (ss - h) - wn * (sn + h))
        return own, wb * (sb + h), wa * (h - sa), ws * (ss + h), wn * (h - sn)

    def opening(o, wet, beyond=False):
        row = o + sub
        shut = ((row < R0) & (lon == 0)) | ((row >= R1) & (lon == nlon - 1)) | beyond
        return jnp.where(shut, 0.0, jnp.where(ocean, wet, 1.0))

    def coefficients(o, rows):
        before, after = pl.ds(o - 1, 8), pl.ds(o + 1, 8)
        w, wb, wa = opening(o, f0[WET, rows]), opening(o - 1, f0[WET, before]), opening(o + 1, f0[WET, after])
        above = None
        for k in range(K):
            u, ub, ua = f0[U + k, rows], f0[U + k, before], f0[U + k, after]
            own, *others = faces(mix[0, level(k)], w, wb, wa, u, ub, ua, f0[V + k, rows])
            for j in range(4):
                c[1 + j, k, rows] = others[j]
            if k > 0:
                own = own - above
            if k < K - 1:
                above = w * number(k)
                c[5, k + 1, rows] = above
                own = own - above
            c[0, k, rows] = own

    def inner(i, carry):
        @pl.when(i == 3)
        def _():
            for n in range(len(near)):
                arrived(n)

        o = pl.multiple_of(jnp.where(i < 3, 16 + 8 * i, 8 + 32 * (i - 3)), 8)
        rows = pl.ds(o, 8)
        for ch in range(T + 2):
            x = own_edges(ch, rows)
            if ch < T:
                sw0[ch, rows], se0[ch, rows] = x, x
            else:
                uw[ch - T, rows], ue[ch - T, rows] = x, x
        coefficients(o, rows)
        return carry

    lax.fori_loop(0, 5, inner, 0)

    share = jnp.where(ocean, OCEAN_SHARE, 1.0)

    def repeat(x):
        x = x + turn(x, SLOT)
        x = x + turn(x, 2 * SLOT)
        return x + turn(x, 4 * SLOT)

    def outer(i, carry):
        o = 8 + 8 * i
        rows = pl.ds(pl.multiple_of(o, 8), 8)
        for ch in range(T + 2):
            q, m = ch // 4, ch % 4
            west, east = (sw0.at[ch], se0.at[ch]) if ch < T else (uw.at[ch - T], ue.at[ch - T])
            west[rows] = jnp.where(far_w, turn(rw[q, rows], -W * m), west[rows])
            east[rows] = jnp.where(far_e, turn(re[q, rows], W - W * m), east[rows])
        wet, transfer = turn(f0[WET, rows], W), turn(f0[TRANSFER, rows], W)
        first = slot == 0
        for r, fields, far, at, beyond in ((rw, uw, far_w & first, 0, lat == 0), (re, ue, far_e & first, W, lat == nlat - 1)):
            ours = between(lane, W, 2 * W) if r is rw else between(ahead, 0, 2 * W)
            near_wet = jnp.where(far, turn(r[2, rows], at), jnp.where(ours, wet, 0.0))
            gain = jnp.where(far, turn(r[2, rows], at - W), jnp.where(ours, transfer, 0.0))
            fields[2, rows] = opening(o, repeat(near_wet), (far_w if r is rw else far_e) & beyond)
            fields[3, rows] = share * gain * near_wet
        return carry

    lax.fori_loop(0, 5, outer, 0)

    def edges(i, carry):
        o = 8 + 8 * i
        rows, before, after = pl.ds(pl.multiple_of(o, 8), 8), pl.ds(o - 1, 8), pl.ds(o + 1, 8)
        for side, (fields, cs) in enumerate(((uw, cw), (ue, ce))):
            w = fields[2, rows]
            up, down = w * hs[side, 1], w * hs[side, 2]
            u = [fields[0, r] for r in (rows, before, after)]
            own, *others = faces(hs[side, 0], w, fields[2, before], fields[2, after], *u, fields[1, rows])
            for j, x in enumerate((own - up - down, *others, up, down)):
                cs[j, rows] = x
        return carry

    lax.fori_loop(0, 5, edges, 0)
    for n in range(len(near)):
        sent(n)

    def stencil(src, k, o):
        rows, before, after = pl.ds(o, 8), pl.ds(o - 1, 8), pl.ds(o + 1, 8)
        co, cb, ca, cs, cn = (c[j, k, rows] for j in range(5))
        up, down = c[5, k, rows], c[5, k + 1, rows]
        for t in range(T):
            p = SURFACE + T * k + t
            x = src[p, rows]
            y = co * x + cb * src[p, before] + ca * src[p, after]
            y = y + (cs * turn(x, 1) + cn * turn(x, -1))
            yield t, y + (up * src[p - T, rows] + down * src[p + T, rows])

    def substep(src, dst, first, pairs):
        def one(n, carry):
            for k in (first + 2 * n, first + 2 * n + 1):
                for i in range(5):
                    o = 8 + 8 * i
                    for t, y in stencil(src, k, o):
                        dst[SURFACE + T * k + t, pl.ds(o, 8)] = y
            return carry

        lax.fori_loop(0, pairs, one, 0)

    def strip_substep(west, east, wnext, enext):
        def some(half, carry):
            for i in range(5):
                o = 8 + 8 * i
                rows, before, after = pl.ds(o, 8), pl.ds(o - 1, 8), pl.ds(o + 1, 8)
                for src, dst, cs in ((west, wnext, cw), (east, enext, ce)):
                    co, cb, ca, cl, cr, up, down = (cs[j, rows] for j in range(7))
                    for t in range(T // 2):
                        t = half * (T // 2) + t
                        x = src[t, rows]
                        y = co * x + cb * src[t, before] + ca * src[t, after]
                        y = y + (cl * turn(x, 1) + cr * turn(x, -1))
                        dst[t, rows] = y + (up * turn(x, SLOT) + down * turn(x, -SLOT))
            return carry

        lax.fori_loop(0, 2, some, 0)

    def finish(n, carry):
        stale = (lane < W) | (lane >= CY - W)
        for k in (2 * n, 2 * n + 1):
            for i in range(CX // 8):
                o = R0 + 8 * i
                for t, y in stencil(f3, k, o):
                    fresh = jnp.where(far_w, se0[t, pl.ds(o, 8)], sw0[t, pl.ds(o, 8)])
                    fresh = pltpu.roll(fresh, CY - W - SLOT * k, 1)
                    out[0, t, level(k), pl.ds(8 * i, 8)] = jnp.where(stale, fresh, y)
        return carry

    def exchange(i, carry):
        rows = pl.ds(pl.multiple_of(8 + 8 * i, 8), 8)
        gain = share * f0[TRANSFER, rows] * f0[WET, rows]
        for t in range(T):
            x = f0[SURFACE + t, rows]
            f0[SURFACE + t, rows] = x + gain * (f0[t, rows] - x)
        for t in range(T):
            theirs = turn(f0[t, rows], W)
            west = jnp.where(far_w, turn(rw[3, rows], -W * (t + 2)), theirs)
            east = jnp.where(far_e, turn(re[3, rows], -W * (t + 1)), theirs)
            for s, fields, x in ((sw0, uw, west), (se0, ue, east)):
                s[t, rows] = s[t, rows] + fields[3, rows] * (x - s[t, rows])
        return carry

    def phase(late, carry):
        @pl.when(late == 1)
        def _():
            for n in range(len(near), len(messages)):
                sent(n)
            for n in range(len(near), len(messages)):
                arrived(n)
            lax.fori_loop(0, 5, exchange, 0)

        early = 1 - late
        substep(f0, f1, 2 * early, 1 + 2 * early)
        substep(f1, f2, 2 * early, 2 + early)
        substep(f2, f3, 4 * early, 2)
        return carry

    lax.fori_loop(0, 2, phase, 0)

    def strips(j, carry):
        strip_substep(sw0, se0, sw1, se1)
        strip_substep(sw1, se1, sw0, se0)
        return carry

    lax.fori_loop(0, SUBSTEPS // 2, strips, 0)
    lax.fori_loop(0, K // 2, finish, 0)


N_MESSAGES = 17


def body(tracer, velocity, mixing, vertical_mixing, transfer_coef, land_mask):
    f32 = jnp.float32
    anywhere = pl.BlockSpec(memory_space=pl.ANY)
    scalars = pl.BlockSpec(memory_space=pltpu.SMEM)

    def planes(*n):
        return pltpu.VMEM((*n, ROWS, CY), f32)

    return pl.pallas_call(
        kernel,
        out_shape=pltpu.VMEM(tracer.shape, f32),
        in_specs=[anywhere, anywhere, scalars, scalars, anywhere, anywhere],
        out_specs=pl.BlockSpec(memory_space=pltpu.VMEM),
        scratch_shapes=[
            planes(PLANES),
            *[planes(T * (K + 2))] * 3,
            *[planes(T)] * 4,
            *[planes(3)] * 2,
            *[planes(4)] * 4,
            planes(6, K + 1),
            *[planes(7)] * 2,
            pltpu.VMEM((2, 3, 8, CY), f32),
            pltpu.VMEM((CX, CY), jnp.int32),
            pltpu.SemaphoreType.DMA((2,)),
            pltpu.SemaphoreType.DMA((N_MESSAGES,)),
            pltpu.SemaphoreType.DMA((N_MESSAGES,)),
        ],
        compiler_params=pltpu.CompilerParams(collective_id=0, has_side_effects=True),
        name="interval",
    )(tracer, velocity, mixing, vertical_mixing, transfer_coef, land_mask)


def solution(mesh):
    return jax.shard_map(
        body,
        mesh=mesh,
        in_specs=(
            P("grp", None, None, "lon", "lat"),
            P("grp", None, None, "lon", "lat"),
            P("grp", None),
            P("grp", None),
            P("lon", "lat"),
            P("lon", "lat"),
        ),
        out_specs=P("grp", None, None, "lon", "lat"),
        check_vma=False,
    )
```

```python
import jax
import jax.numpy as jnp
from jax import lax
from jax.experimental import pallas as pl
from jax.experimental.pallas import tpu as pltpu
from jax.sharding import PartitionSpec as P

SUBSTEPS = 4
OCEAN_SHARE = 0.5
T = 6
K = 8
CX, CY = 32, 128
R0, R1 = 12, 44
ROWS = 56
W = 4
SLOT = 16
OWN = 8
SURFACE, U, V, WET, TRANSFER, PLANES = T, T + T * K, T + T * K + K, 70, 71, 72
MESH = pl.DeviceIdType.MESH


def kernel(tr, vel, mix, vmx, coef, mask, out, f0, f1, f2, f3, sw0, sw1, se0, se1, pw, pe, rw, re, uw, ue, c, cw, ce, hs, msk, lsem, ssem, rsem):
    grp, lon, lat = lax.axis_index("grp"), lax.axis_index("lon"), lax.axis_index("lat")
    nlon, nlat = lax.axis_size("lon"), lax.axis_size("lat")
    ocean = grp == 1

    def exists(di, dj, sign=1):
        ok = None
        for pos, size, d in ((lon, nlon, di * sign), (lat, nlat, dj * sign)):
            if d:
                one = pos < size - 1 if d > 0 else pos > 0
                ok = one if ok is None else jnp.logical_and(ok, one)
        return ok

    def device(dg, di, dj):
        return {"grp": grp if dg == 0 else 1 - grp, "lon": lon + di, "lat": lat + dj}

    def guarded(ok, act):
        if ok is None:
            act()
        else:
            pl.when(ok)(act)

    barrier = pltpu.get_barrier_semaphore()
    places = [(1, a, b) for a in (1, -1) for b in (1, -1)]
    places += [(0, a, b) for a in (1, -1) for b in (1, -1)]
    places += [(1, 1, 0), (1, -1, 0), (1, 0, 1), (1, 0, -1)]
    places += [(1, 0, 0), (0, 0, 1), (0, 0, -1), (0, 1, 0), (0, -1, 0)]
    for where in places:

        def greet(where=where):
            pl.semaphore_signal(barrier, inc=1, device_id=device(*where), device_id_type=MESH)

        guarded(exists(*where[1:]), greet)
    beside = (lon > 0).astype(jnp.int32) + (lon < nlon - 1).astype(jnp.int32)
    along = (lat > 0).astype(jnp.int32) + (lat < nlat - 1).astype(jnp.int32)
    met = 2 * (1 + beside) * (1 + along) - 1

    def level(k):
        return jnp.where(ocean, k, K - 1 - k)

    lo, hi, mid = pl.ds(R0, W), pl.ds(R1 - W, W), pl.ds(R0, CX)
    inlo, inhi = pl.ds(R0 - W, W), pl.ds(R1, W)

    def fetch(k, carry):
        pltpu.make_async_copy(tr.at[0, :, level(k)], f0.at[pl.ds(SURFACE + T * k, T), mid], lsem.at[0]).start()
        pltpu.make_async_copy(vel.at[0, 0, level(k)], f0.at[U + k, mid], lsem.at[0]).start()
        pltpu.make_async_copy(vel.at[0, 1, level(k)], f0.at[V + k, mid], lsem.at[0]).start()
        return carry

    pltpu.make_async_copy(mask, msk, lsem.at[1]).start()
    pltpu.make_async_copy(coef, f0.at[TRANSFER, mid], lsem.at[0]).start()
    lax.fori_loop(0, K, fetch, 0)

    def clear(ref, n, first, count):
        def one(j, carry):
            ref[j, pl.ds(first, count)] = jnp.zeros((count, CY), jnp.float32)
            return carry

        lax.fori_loop(0, n, one, 0)

    @pl.when(lon == 0)
    def _():
        clear(f0, PLANES, R0 - W, W), clear(rw, 4, R0 - W, W), clear(re, 4, R0 - W, W)

    @pl.when(lon == nlon - 1)
    def _():
        clear(f0, PLANES, R1, W), clear(rw, 4, R1, W), clear(re, 4, R1, W)

    @pl.when(lat == 0)
    def _():
        clear(rw, 4, R0 - W, CX + 2 * W)

    @pl.when(lat == nlat - 1)
    def _():
        clear(re, 4, R0 - W, CX + 2 * W)

    lane = lax.broadcasted_iota(jnp.int32, (8, CY), 1)
    sub = lax.broadcasted_iota(jnp.int32, (8, CY), 0)
    zero = jnp.zeros((8, CY), jnp.float32)
    ahead = (lane + W) % CY
    slot = ahead // SLOT
    part = (lane % SLOT) // W
    far_w, far_e = part == 0, part == 1
    def turn(x, shift):
        shift = shift % CY
        return x if shift == 0 else pltpu.roll(x, shift, 1)

    def between(x, a, n):
        return (x >= a) & (x < a + n)

    pltpu.make_async_copy(mask, msk, lsem.at[1]).wait()
    total = pl.ds(0, T * K + 2 * K + 1)
    pltpu.make_async_copy(f0.at[total, mid], f0.at[total, mid], lsem.at[0]).wait()
    f0[WET, mid] = msk[...].astype(jnp.float32)

    def own_edges(ch, rows):
        acc = zero
        for k in range(K):
            x = f0[SURFACE + T * k + ch if ch < T else U + K * (ch - T) + k, rows]
            acc = jnp.where(slot == k, turn(x, SLOT * k + W), acc)
        return acc

    def pack(i, carry):
        rows = pl.ds(R0 + 8 * i, 8)
        west, east = [zero, zero, zero], [zero, zero, zero]
        for ch in range(T + 2):
            x, q, m = own_edges(ch, rows), ch // 4, ch % 4
            west[q] = jnp.where(part == m, turn(x, W * m), west[q])
            east[q] = jnp.where(part == m, turn(x, W * m - W), east[q])
            if ch < T:
                put = between(lane, W * (ch + 2), W)
                west[2] = jnp.where(put, turn(x, W * (ch + 2)), west[2])
                east[2] = jnp.where(put, turn(x, W * (ch + 1)), east[2])
        for j, plane in enumerate((WET, TRANSFER)):
            x, put = f0[plane, rows], between(lane, W * j, W)
            west[2] = jnp.where(put, turn(x, W * (j + 1)), west[2])
            east[2] = jnp.where(put, turn(x, W * j), east[2])
        for q in range(3):
            pw[q, rows], pe[q, rows] = west[q], east[q]
        return carry

    lax.fori_loop(0, CX // 8, pack, 0)

    near, far = [], []
    for dj, p, r in ((1, pw, rw), (-1, pe, re)):
        packs = pl.ds(0, 3)
        near.append(((0, 0, dj), p.at[packs, mid], r.at[packs, mid]))
        near.append(((0, 1, dj), p.at[packs, hi], r.at[packs, inlo]))
        near.append(((0, -1, dj), p.at[packs, lo], r.at[packs, inhi]))
        far.append(((1, 0, dj), p.at[2, mid], r.at[3, mid]))
        far.append(((1, 1, dj), p.at[2, hi], r.at[3, inlo]))
        far.append(((1, -1, dj), p.at[2, lo], r.at[3, inhi]))
    block = pl.ds(SURFACE, PLANES - SURFACE)
    near.append(((0, 1, 0), f0.at[block, hi], f0.at[block, inlo]))
    near.append(((0, -1, 0), f0.at[block, lo], f0.at[block, inhi]))
    surface, other = pl.ds(SURFACE, T), pl.ds(0, T)
    far.append(((1, 1, 0), f0.at[surface, hi], f0.at[other, inlo]))
    far.append(((1, -1, 0), f0.at[surface, lo], f0.at[other, inhi]))
    far.append(((1, 0, 0), f0.at[surface, mid], f0.at[other, mid]))
    messages = near + far

    def remote(n):
        where, src, dst = messages[n]
        return pltpu.make_async_remote_copy(
            src_ref=src, dst_ref=dst, send_sem=ssem.at[n], recv_sem=rsem.at[n], device_id=device(*where), device_id_type=MESH
        )

    def arrived(n):
        guarded(exists(*messages[n][0][1:], sign=-1), lambda: remote(n).wait_recv())

    def sent(n):
        guarded(exists(*messages[n][0][1:]), lambda: remote(n).wait_send())

    pl.semaphore_wait(barrier, met)
    for n in [0, 3, 1, 2, 4, 5, 6, 7, 16, 9, 10, 12, 13, 14, 15, 8, 11]:
        guarded(exists(*messages[n][0][1:]), lambda n=n: remote(n).start())

    def pads(i, carry):
        rows = pl.ds(pl.multiple_of(8 + 8 * i, 8), 8)
        for f in (f1, f2, f3):
            for t in range(T):
                f[t, rows] = zero
                f[T + T * K + t, rows] = zero
        c[5, 0, rows] = zero
        c[5, K, rows] = zero
        return carry

    lax.fori_loop(0, 5, pads, 0)

    def number(k):
        return vmx[0, jnp.where(ocean, k, K - 2 - k)]

    for side, its in enumerate((lane // SLOT, slot)):
        h, up, down = zero, zero, zero
        for k in range(K):
            h = jnp.where(its == k, mix[0, level(k)], h)
            if k > 0:
                up = jnp.where(its == k, number(k - 1), up)
            if k < K - 1:
                down = jnp.where(its == k, number(k), down)
        hs[side, 0], hs[side, 1], hs[side, 2] = h, up, down

    def faces(h, w, wb, wa, u, ub, ua, v):
        wb, wa = w * wb, w * wa
        ws, wn = w * turn(w, 1), w * turn(w, -1)
        sb, sa = 0.25 * (ub + u), 0.25 * (ua + u)
        ss, sn = 0.25 * (turn(v, 1) + v), 0.25 * (turn(v, -1) + v)
        own = 1.0 + (wb * (sb - h) - wa * (sa + h)) + (ws * (ss - h) - wn * (sn + h))
        return own, wb * (sb + h), wa * (h - sa), ws * (ss + h), wn * (h - sn)

    def opening(o, wet, beyond=False):
        row = o + sub
        shut = ((row < R0) & (lon == 0)) | ((row >= R1) & (lon == nlon - 1)) | beyond
        return jnp.where(shut, 0.0, jnp.where(ocean, wet, 1.0))

    def coefficients(o, rows):
        before, after = pl.ds(o - 1, 8), pl.ds(o + 1, 8)
        w, wb, wa = opening(o, f0[WET, rows]), opening(o - 1, f0[WET, before]), opening(o + 1, f0[WET, after])
        above = None
        for k in range(K):
            u, ub, ua = f0[U + k, rows], f0[U + k, before], f0[U + k, after]
            own, *others = faces(mix[0, level(k)], w, wb, wa, u, ub, ua, f0[V + k, rows])
            for j in range(4):
                c[1 + j, k, rows] = others[j]
            if k > 0:
                own = own - above
            if k < K - 1:
                above = w * number(k)
                c[5, k + 1, rows] = above
                own = own - above
            c[0, k, rows] = own

    def inner(i, carry):
        @pl.when(i == 3)
        def _():
            for n in range(len(near)):
                arrived(n)

        o = pl.multiple_of(jnp.where(i < 3, 16 + 8 * i, 8 + 32 * (i - 3)), 8)
        rows = pl.ds(o, 8)
        for ch in range(T + 2):
            x = own_edges(ch, rows)
            if ch < T:
                sw0[ch, rows], se0[ch, rows] = x, x
            else:
                uw[ch - T, rows], ue[ch - T, rows] = x, x
        coefficients(o, rows)
        return carry

    lax.fori_loop(0, 5, inner, 0)

    share = jnp.where(ocean, OCEAN_SHARE, 1.0)

    def repeat(x):
        x = x + turn(x, SLOT)
        x = x + turn(x, 2 * SLOT)
        return x + turn(x, 4 * SLOT)

    def outer(i, carry):
        o = 8 + 8 * i
        rows = pl.ds(pl.multiple_of(o, 8), 8)
        for ch in range(T + 2):
            q, m = ch // 4, ch % 4
            west, east = (sw0.at[ch], se0.at[ch]) if ch < T else (uw.at[ch - T], ue.at[ch - T])
            west[rows] = jnp.where(far_w, turn(rw[q, rows], -W * m), west[rows])
            east[rows] = jnp.where(far_e, turn(re[q, rows], W - W * m), east[rows])
        wet, transfer = turn(f0[WET, rows], W), turn(f0[TRANSFER, rows], W)
        first = slot == 0
        for r, fields, far, at, beyond in ((rw, uw, far_w & first, 0, lat == 0), (re, ue, far_e & first, W, lat == nlat - 1)):
            ours = between(lane, W, 2 * W) if r is rw else between(ahead, 0, 2 * W)
            near_wet = jnp.where(far, turn(r[2, rows], at), jnp.where(ours, wet, 0.0))
            gain = jnp.where(far, turn(r[2, rows], at - W), jnp.where(ours, transfer, 0.0))
            fields[2, rows] = opening(o, repeat(near_wet), (far_w if r is rw else far_e) & beyond)
            fields[3, rows] = share * gain * near_wet
        return carry

    lax.fori_loop(0, 5, outer, 0)

    def edges(i, carry):
        o = 8 + 8 * i
        rows, before, after = pl.ds(pl.multiple_of(o, 8), 8), pl.ds(o - 1, 8), pl.ds(o + 1, 8)
        for side, (fields, cs) in enumerate(((uw, cw), (ue, ce))):
            w = fields[2, rows]
            up, down = w * hs[side, 1], w * hs[side, 2]
            u = [fields[0, r] for r in (rows, before, after)]
            own, *others = faces(hs[side, 0], w, fields[2, before], fields[2, after], *u, fields[1, rows])
            for j, x in enumerate((own - up - down, *others, up, down)):
                cs[j, rows] = x
        return carry

    lax.fori_loop(0, 5, edges, 0)
    for n in range(len(near)):
        sent(n)

    def stencil(src, k, o):
        rows, before, after = pl.ds(o, 8), pl.ds(o - 1, 8), pl.ds(o + 1, 8)
        co, cb, ca, cs, cn = (c[j, k, rows] for j in range(5))
        up, down = c[5, k, rows], c[5, k + 1, rows]
        for t in range(T):
            p = SURFACE + T * k + t
            x = src[p, rows]
            y = co * x + cb * src[p, before] + ca * src[p, after]
            y = y + (cs * turn(x, 1) + cn * turn(x, -1))
            yield t, y + (up * src[p - T, rows] + down * src[p + T, rows])

    def substep(src, dst, first, pairs):
        def one(n, carry):
            for k in (first + 2 * n, first + 2 * n + 1):
                for i in range(5):
                    o = 8 + 8 * i
                    for t, y in stencil(src, k, o):
                        dst[SURFACE + T * k + t, pl.ds(o, 8)] = y
            return carry

        lax.fori_loop(0, pairs, one, 0)

    def strip_substep(west, east, wnext, enext):
        if True:
            for i in range(5):
                o = 8 + 8 * i
                rows, before, after = pl.ds(o, 8), pl.ds(o - 1, 8), pl.ds(o + 1, 8)
                for src, dst, cs in ((west, wnext, cw), (east, enext, ce)):
                    co, cb, ca, cl, cr, up, down = (cs[j, rows] for j in range(7))
                    for t in range(T):
                        x = src[t, rows]
                        y = co * x + cb * src[t, before] + ca * src[t, after]
                        y = y + (cl * turn(x, 1) + cr * turn(x, -1))
                        dst[t, rows] = y + (up * turn(x, SLOT) + down * turn(x, -SLOT))

    def finish(n, carry):
        stale = (lane < W) | (lane >= CY - W)
        for k in (2 * n, 2 * n + 1):
            for i in range(CX // 8):
                o = R0 + 8 * i
                for t, y in stencil(f3, k, o):
                    fresh = jnp.where(far_w, se0[t, pl.ds(o, 8)], sw0[t, pl.ds(o, 8)])
                    fresh = pltpu.roll(fresh, CY - W - SLOT * k, 1)
                    out[0, t, level(k), pl.ds(8 * i, 8)] = jnp.where(stale, fresh, y)
        return carry

    def exchange(i, carry):
        rows = pl.ds(pl.multiple_of(8 + 8 * i, 8), 8)
        gain = share * f0[TRANSFER, rows] * f0[WET, rows]
        for t in range(T):
            x = f0[SURFACE + t, rows]
            f0[SURFACE + t, rows] = x + gain * (f0[t, rows] - x)
        for t in range(T):
            theirs = turn(f0[t, rows], W)
            west = jnp.where(far_w, turn(rw[3, rows], -W * (t + 2)), theirs)
            east = jnp.where(far_e, turn(re[3, rows], -W * (t + 1)), theirs)
            for s, fields, x in ((sw0, uw, west), (se0, ue, east)):
                s[t, rows] = s[t, rows] + fields[3, rows] * (x - s[t, rows])
        return carry

    def phase(late, carry):
        @pl.when(late == 1)
        def _():
            for n in range(len(near), len(messages)):
                sent(n)
            for n in range(len(near), len(messages)):
                arrived(n)
            lax.fori_loop(0, 5, exchange, 0)

        early = 1 - late
        substep(f0, f1, 2 * early, 1 + 2 * early)
        substep(f1, f2, 2 * early, 2 + early)
        substep(f2, f3, 4 * early, 2)
        return carry

    lax.fori_loop(0, 2, phase, 0)

    def strips(j, carry):
        strip_substep(sw0, se0, sw1, se1)
        strip_substep(sw1, se1, sw0, se0)
        return carry

    lax.fori_loop(0, SUBSTEPS // 2, strips, 0)
    lax.fori_loop(0, K // 2, finish, 0)


N_MESSAGES = 17


def body(tracer, velocity, mixing, vertical_mixing, transfer_coef, land_mask):
    f32 = jnp.float32
    anywhere = pl.BlockSpec(memory_space=pl.ANY)
    scalars = pl.BlockSpec(memory_space=pltpu.SMEM)

    def planes(*n):
        return pltpu.VMEM((*n, ROWS, CY), f32)

    return pl.pallas_call(
        kernel,
        out_shape=pltpu.VMEM(tracer.shape, f32),
        in_specs=[anywhere, anywhere, scalars, scalars, anywhere, anywhere],
        out_specs=pl.BlockSpec(memory_space=pltpu.VMEM),
        scratch_shapes=[
            planes(PLANES),
            *[planes(T * (K + 2))] * 3,
            *[planes(T)] * 4,
            *[planes(3)] * 2,
            *[planes(4)] * 4,
            planes(6, K + 1),
            *[planes(7)] * 2,
            pltpu.VMEM((2, 3, 8, CY), f32),
            pltpu.VMEM((CX, CY), jnp.int32),
            pltpu.SemaphoreType.DMA((2,)),
            pltpu.SemaphoreType.DMA((N_MESSAGES,)),
            pltpu.SemaphoreType.DMA((N_MESSAGES,)),
        ],
        compiler_params=pltpu.CompilerParams(collective_id=0, has_side_effects=True),
        name="interval",
    )(tracer, velocity, mixing, vertical_mixing, transfer_coef, land_mask)


def solution(mesh):
    return jax.shard_map(
        body,
        mesh=mesh,
        in_specs=(
            P("grp", None, None, "lon", "lat"),
            P("grp", None, None, "lon", "lat"),
            P("grp", None),
            P("grp", None),
            P("lon", "lat"),
            P("lon", "lat"),
        ),
        out_specs=P("grp", None, None, "lon", "lat"),
        check_vma=False,
    )
```

```python
import jax
import jax.numpy as jnp
from jax import lax
from jax.experimental import pallas as pl
from jax.experimental.pallas import tpu as pltpu
from jax.sharding import PartitionSpec as P

SUBSTEPS = 4
OCEAN_SHARE = 0.5
T = 6
K = 8
CX, CY = 32, 128
R0, R1 = 12, 44
ROWS = 56
W = 4
SLOT = 16
OWN = 8
SURFACE, U, V, WET, TRANSFER, PLANES = T, T + T * K, T + T * K + K, 70, 71, 72
MESH = pl.DeviceIdType.MESH


def kernel(tr, vel, mix, vmx, coef, mask, out, f0, f1, f2, f3, sw0, sw1, se0, se1, pw, pe, rw, re, uw, ue, c, cw, ce, hs, msk, lsem, ssem, rsem):
    grp, lon, lat = lax.axis_index("grp"), lax.axis_index("lon"), lax.axis_index("lat")
    nlon, nlat = lax.axis_size("lon"), lax.axis_size("lat")
    ocean = grp == 1

    def exists(di, dj, sign=1):
        ok = None
        for pos, size, d in ((lon, nlon, di * sign), (lat, nlat, dj * sign)):
            if d:
                one = pos < size - 1 if d > 0 else pos > 0
                ok = one if ok is None else jnp.logical_and(ok, one)
        return ok

    def device(dg, di, dj):
        return {"grp": grp if dg == 0 else 1 - grp, "lon": lon + di, "lat": lat + dj}

    def guarded(ok, act):
        if ok is None:
            act()
        else:
            pl.when(ok)(act)

    barrier = pltpu.get_barrier_semaphore()
    places = [(1, a, b) for a in (1, -1) for b in (1, -1)]
    places += [(0, a, b) for a in (1, -1) for b in (1, -1)]
    places += [(1, 1, 0), (1, -1, 0), (1, 0, 1), (1, 0, -1)]
    places += [(1, 0, 0), (0, 0, 1), (0, 0, -1), (0, 1, 0), (0, -1, 0)]
    for where in places:

        def greet(where=where):
            pl.semaphore_signal(barrier, inc=1, device_id=device(*where), device_id_type=MESH)

        guarded(exists(*where[1:]), greet)
    beside = (lon > 0).astype(jnp.int32) + (lon < nlon - 1).astype(jnp.int32)
    along = (lat > 0).astype(jnp.int32) + (lat < nlat - 1).astype(jnp.int32)
    met = 2 * (1 + beside) * (1 + along) - 1

    def level(k):
        return jnp.where(ocean, k, K - 1 - k)

    lo, hi, mid = pl.ds(R0, W), pl.ds(R1 - W, W), pl.ds(R0, CX)
    inlo, inhi = pl.ds(R0 - W, W), pl.ds(R1, W)

    def fetch(k, carry):
        pltpu.make_async_copy(tr.at[0, :, level(k)], f0.at[pl.ds(SURFACE + T * k, T), mid], lsem.at[0]).start()
        pltpu.make_async_copy(vel.at[0, 0, level(k)], f0.at[U + k, mid], lsem.at[0]).start()
        pltpu.make_async_copy(vel.at[0, 1, level(k)], f0.at[V + k, mid], lsem.at[0]).start()
        return carry

    pltpu.make_async_copy(mask, msk, lsem.at[1]).start()
    pltpu.make_async_copy(coef, f0.at[TRANSFER, mid], lsem.at[0]).start()
    lax.fori_loop(0, K, fetch, 0)

    def clear(ref, n, first, count):
        def one(j, carry):
            ref[j, pl.ds(first, count)] = jnp.zeros((count, CY), jnp.float32)
            return carry

        lax.fori_loop(0, n, one, 0)

    @pl.when(lon == 0)
    def _():
        clear(f0, PLANES, R0 - W, W), clear(rw, 4, R0 - W, W), clear(re, 4, R0 - W, W)

    @pl.when(lon == nlon - 1)
    def _():
        clear(f0, PLANES, R1, W), clear(rw, 4, R1, W), clear(re, 4, R1, W)

    @pl.when(lat == 0)
    def _():
        clear(rw, 4, R0 - W, CX + 2 * W)

    @pl.when(lat == nlat - 1)
    def _():
        clear(re, 4, R0 - W, CX + 2 * W)

    lane = lax.broadcasted_iota(jnp.int32, (8, CY), 1)
    sub = lax.broadcasted_iota(jnp.int32, (8, CY), 0)
    zero = jnp.zeros((8, CY), jnp.float32)
    ahead = (lane + W) % CY
    slot = ahead // SLOT
    part = (lane % SLOT) // W
    far_w, far_e = part == 0, part == 1
    def turn(x, shift):
        shift = shift % CY
        return x if shift == 0 else pltpu.roll(x, shift, 1)

    def between(x, a, n):
        return (x >= a) & (x < a + n)

    pltpu.make_async_copy(mask, msk, lsem.at[1]).wait()
    total = pl.ds(0, T * K + 2 * K + 1)
    pltpu.make_async_copy(f0.at[total, mid], f0.at[total, mid], lsem.at[0]).wait()
    f0[WET, mid] = msk[...].astype(jnp.float32)

    def own_edges(ch, rows):
        acc = zero
        for k in range(K):
            x = f0[SURFACE + T * k + ch if ch < T else U + K * (ch - T) + k, rows]
            acc = jnp.where(slot == k, turn(x, SLOT * k + W), acc)
        return acc

    def pack(i, carry):
        rows = pl.ds(R0 + 8 * i, 8)
        west, east = [zero, zero, zero], [zero, zero, zero]
        for ch in range(T + 2):
            x, q, m = own_edges(ch, rows), ch // 4, ch % 4
            west[q] = jnp.where(part == m, turn(x, W * m), west[q])
            east[q] = jnp.where(part == m, turn(x, W * m - W), east[q])
            if ch < T:
                put = between(lane, W * (ch + 2), W)
                west[2] = jnp.where(put, turn(x, W * (ch + 2)), west[2])
                east[2] = jnp.where(put, turn(x, W * (ch + 1)), east[2])
        for j, plane in enumerate((WET, TRANSFER)):
            x, put = f0[plane, rows], between(lane, W * j, W)
            west[2] = jnp.where(put, turn(x, W * (j + 1)), west[2])
            east[2] = jnp.where(put, turn(x, W * j), east[2])
        for q in range(3):
            pw[q, rows], pe[q, rows] = west[q], east[q]
        return carry

    lax.fori_loop(0, CX // 8, pack, 0)

    near, far = [], []
    for dj, p, r in ((1, pw, rw), (-1, pe, re)):
        packs = pl.ds(0, 3)
        near.append(((0, 0, dj), p.at[packs, mid], r.at[packs, mid]))
        near.append(((0, 1, dj), p.at[packs, hi], r.at[packs, inlo]))
        near.append(((0, -1, dj), p.at[packs, lo], r.at[packs, inhi]))
        far.append(((1, 0, dj), p.at[2, mid], r.at[3, mid]))
        far.append(((1, 1, dj), p.at[2, hi], r.at[3, inlo]))
        far.append(((1, -1, dj), p.at[2, lo], r.at[3, inhi]))
    block = pl.ds(SURFACE, PLANES - SURFACE)
    near.append(((0, 1, 0), f0.at[block, hi], f0.at[block, inlo]))
    near.append(((0, -1, 0), f0.at[block, lo], f0.at[block, inhi]))
    surface, other = pl.ds(SURFACE, T), pl.ds(0, T)
    far.append(((1, 1, 0), f0.at[surface, hi], f0.at[other, inlo]))
    far.append(((1, -1, 0), f0.at[surface, lo], f0.at[other, inhi]))
    far.append(((1, 0, 0), f0.at[surface, mid], f0.at[other, mid]))
    messages = near + far

    def remote(n):
        where, src, dst = messages[n]
        return pltpu.make_async_remote_copy(
            src_ref=src, dst_ref=dst, send_sem=ssem.at[n], recv_sem=rsem.at[n], device_id=device(*where), device_id_type=MESH
        )

    def arrived(n):
        guarded(exists(*messages[n][0][1:], sign=-1), lambda: remote(n).wait_recv())

    def sent(n):
        guarded(exists(*messages[n][0][1:]), lambda: remote(n).wait_send())

    pl.semaphore_wait(barrier, met)
    for n in [0, 3, 1, 2, 4, 5, 9, 10, 12, 13, 6, 7, 16, 14, 15, 8, 11]:
        guarded(exists(*messages[n][0][1:]), lambda n=n: remote(n).start())

    def pads(i, carry):
        rows = pl.ds(pl.multiple_of(8 + 8 * i, 8), 8)
        for f in (f1, f2, f3):
            for t in range(T):
                f[t, rows] = zero
                f[T + T * K + t, rows] = zero
        c[5, 0, rows] = zero
        c[5, K, rows] = zero
        return carry

    lax.fori_loop(0, 5, pads, 0)

    def number(k):
        return vmx[0, jnp.where(ocean, k, K - 2 - k)]

    for side, its in enumerate((lane // SLOT, slot)):
        h, up, down = zero, zero, zero
        for k in range(K):
            h = jnp.where(its == k, mix[0, level(k)], h)
            if k > 0:
                up = jnp.where(its == k, number(k - 1), up)
            if k < K - 1:
                down = jnp.where(its == k, number(k), down)
        hs[side, 0], hs[side, 1], hs[side, 2] = h, up, down

    def faces(h, w, wb, wa, u, ub, ua, v):
        wb, wa = w * wb, w * wa
        ws, wn = w * turn(w, 1), w * turn(w, -1)
        sb, sa = 0.25 * (ub + u), 0.25 * (ua + u)
        ss, sn = 0.25 * (turn(v, 1) + v), 0.25 * (turn(v, -1) + v)
        own = 1.0 + (wb * (sb - h) - wa * (sa + h)) + (ws * (ss - h) - wn * (sn + h))
        return own, wb * (sb + h), wa * (h - sa), ws * (ss + h), wn * (h - sn)

    def opening(o, wet, beyond=False):
        row = o + sub
        shut = ((row < R0) & (lon == 0)) | ((row >= R1) & (lon == nlon - 1)) | beyond
        return jnp.where(shut, 0.0, jnp.where(ocean, wet, 1.0))

    def coefficients(o, rows):
        before, after = pl.ds(o - 1, 8), pl.ds(o + 1, 8)
        w, wb, wa = opening(o, f0[WET, rows]), opening(o - 1, f0[WET, before]), opening(o + 1, f0[WET, after])
        above = None
        for k in range(K):
            u, ub, ua = f0[U + k, rows], f0[U + k, before], f0[U + k, after]
            own, *others = faces(mix[0, level(k)], w, wb, wa, u, ub, ua, f0[V + k, rows])
            for j in range(4):
                c[1 + j, k, rows] = others[j]
            if k > 0:
                own = own - above
            if k < K - 1:
                above = w * number(k)
                c[5, k + 1, rows] = above
                own = own - above
            c[0, k, rows] = own

    def inner(i, carry):
        @pl.when(i == 3)
        def _():
            for n in range(len(near)):
                sent(n)
            for n in range(len(near)):
                arrived(n)

        o = pl.multiple_of(jnp.where(i < 3, 16 + 8 * i, 8 + 32 * (i - 3)), 8)
        rows = pl.ds(o, 8)
        for ch in range(T + 2):
            x = own_edges(ch, rows)
            if ch < T:
                sw0[ch, rows], se0[ch, rows] = x, x
            else:
                uw[ch - T, rows], ue[ch - T, rows] = x, x
        coefficients(o, rows)
        return carry

    lax.fori_loop(0, 5, inner, 0)

    share = jnp.where(ocean, OCEAN_SHARE, 1.0)

    def repeat(x):
        x = x + turn(x, SLOT)
        x = x + turn(x, 2 * SLOT)
        return x + turn(x, 4 * SLOT)

    def outer(i, carry):
        o = 8 + 8 * i
        rows = pl.ds(pl.multiple_of(o, 8), 8)
        for ch in range(T + 2):
            q, m = ch // 4, ch % 4
            west, east = (sw0.at[ch], se0.at[ch]) if ch < T else (uw.at[ch - T], ue.at[ch - T])
            west[rows] = jnp.where(far_w, turn(rw[q, rows], -W * m), west[rows])
            east[rows] = jnp.where(far_e, turn(re[q, rows], W - W * m), east[rows])
        wet, transfer = turn(f0[WET, rows], W), turn(f0[TRANSFER, rows], W)
        first = slot == 0
        for r, fields, far, at, beyond in ((rw, uw, far_w & first, 0, lat == 0), (re, ue, far_e & first, W, lat == nlat - 1)):
            ours = between(lane, W, 2 * W) if r is rw else between(ahead, 0, 2 * W)
            near_wet = jnp.where(far, turn(r[2, rows], at), jnp.where(ours, wet, 0.0))
            gain = jnp.where(far, turn(r[2, rows], at - W), jnp.where(ours, transfer, 0.0))
            fields[2, rows] = opening(o, repeat(near_wet), (far_w if r is rw else far_e) & beyond)
            fields[3, rows] = share * gain * near_wet
        return carry

    lax.fori_loop(0, 5, outer, 0)

    def edges(i, carry):
        o = 8 + 8 * i
        rows, before, after = pl.ds(pl.multiple_of(o, 8), 8), pl.ds(o - 1, 8), pl.ds(o + 1, 8)
        for side, (fields, cs) in enumerate(((uw, cw), (ue, ce))):
            w = fields[2, rows]
            up, down = w * hs[side, 1], w * hs[side, 2]
            u = [fields[0, r] for r in (rows, before, after)]
            own, *others = faces(hs[side, 0], w, fields[2, before], fields[2, after], *u, fields[1, rows])
            for j, x in enumerate((own - up - down, *others, up, down)):
                cs[j, rows] = x
        return carry

    lax.fori_loop(0, 5, edges, 0)

    def stencil(src, k, o):
        rows, before, after = pl.ds(o, 8), pl.ds(o - 1, 8), pl.ds(o + 1, 8)
        co, cb, ca, cs, cn = (c[j, k, rows] for j in range(5))
        up, down = c[5, k, rows], c[5, k + 1, rows]
        for t in range(T):
            p = SURFACE + T * k + t
            x = src[p, rows]
            y = co * x + cb * src[p, before] + ca * src[p, after]
            y = y + (cs * turn(x, 1) + cn * turn(x, -1))
            yield t, y + (up * src[p - T, rows] + down * src[p + T, rows])

    def substep(src, dst, first, pairs):
        def one(n, carry):
            for k in (first + 2 * n, first + 2 * n + 1):
                for i in range(5):
                    o = 8 + 8 * i
                    for t, y in stencil(src, k, o):
                        dst[SURFACE + T * k + t, pl.ds(o, 8)] = y
            return carry

        lax.fori_loop(0, pairs, one, 0)

    def strip_substep(west, east, wnext, enext):
        if True:
            for i in range(5):
                o = 8 + 8 * i
                rows, before, after = pl.ds(o, 8), pl.ds(o - 1, 8), pl.ds(o + 1, 8)
                for src, dst, cs in ((west, wnext, cw), (east, enext, ce)):
                    co, cb, ca, cl, cr, up, down = (cs[j, rows] for j in range(7))
                    for t in range(T):
                        x = src[t, rows]
                        y = co * x + cb * src[t, before] + ca * src[t, after]
                        dst[t, rows] = y + (cl * turn(x, 1) + cr * turn(x, -1))
            for i in range(5):
                o = 8 + 8 * i
                rows, before, after = pl.ds(o, 8), pl.ds(o - 1, 8), pl.ds(o + 1, 8)
                for src, dst, cs in ((west, wnext, cw), (east, enext, ce)):
                    co, cb, ca, cl, cr, up, down = (cs[j, rows] for j in range(7))
                    for t in range(T):
                        x = src[t, rows]
                        dst[t, rows] = dst[t, rows] + (up * turn(x, SLOT) + down * turn(x, -SLOT))

    def finish(n, carry):
        stale = (lane < W) | (lane >= CY - W)
        for k in (2 * n, 2 * n + 1):
            for i in range(CX // 8):
                o = R0 + 8 * i
                for t, y in stencil(f3, k, o):
                    fresh = jnp.where(far_w, se0[t, pl.ds(o, 8)], sw0[t, pl.ds(o, 8)])
                    fresh = pltpu.roll(fresh, CY - W - SLOT * k, 1)
                    out[0, t, level(k), pl.ds(8 * i, 8)] = jnp.where(stale, fresh, y)
        return carry

    def exchange(i, carry):
        rows = pl.ds(pl.multiple_of(8 + 8 * i, 8), 8)
        gain = share * f0[TRANSFER, rows] * f0[WET, rows]
        for t in range(T):
            x = f0[SURFACE + t, rows]
            f0[SURFACE + t, rows] = x + gain * (f0[t, rows] - x)
        for t in range(T):
            theirs = turn(f0[t, rows], W)
            west = jnp.where(far_w, turn(rw[3, rows], -W * (t + 2)), theirs)
            east = jnp.where(far_e, turn(re[3, rows], -W * (t + 1)), theirs)
            for s, fields, x in ((sw0, uw, west), (se0, ue, east)):
                s[t, rows] = s[t, rows] + fields[3, rows] * (x - s[t, rows])
        return carry

    def phase(late, carry):
        @pl.when(late == 1)
        def _():
            for n in range(len(near), len(messages)):
                sent(n)
            for n in range(len(near), len(messages)):
                arrived(n)
            lax.fori_loop(0, 5, exchange, 0)

        early = 1 - late
        substep(f0, f1, 2 * early, 1 + 2 * early)
        substep(f1, f2, 2 * early, 2 + early)
        substep(f2, f3, 4 * early, 2)
        return carry

    lax.fori_loop(0, 2, phase, 0)

    def strips(j, carry):
        strip_substep(sw0, se0, sw1, se1)
        strip_substep(sw1, se1, sw0, se0)
        return carry

    lax.fori_loop(0, SUBSTEPS // 2, strips, 0)
    lax.fori_loop(0, K // 2, finish, 0)


N_MESSAGES = 17


def body(tracer, velocity, mixing, vertical_mixing, transfer_coef, land_mask):
    f32 = jnp.float32
    anywhere = pl.BlockSpec(memory_space=pl.ANY)
    scalars = pl.BlockSpec(memory_space=pltpu.SMEM)

    def planes(*n):
        return pltpu.VMEM((*n, ROWS, CY), f32)

    return pl.pallas_call(
        kernel,
        out_shape=pltpu.VMEM(tracer.shape, f32),
        in_specs=[anywhere, anywhere, scalars, scalars, anywhere, anywhere],
        out_specs=pl.BlockSpec(memory_space=pltpu.VMEM),
        scratch_shapes=[
            planes(PLANES),
            *[planes(T * (K + 2))] * 3,
            *[planes(T)] * 4,
            *[planes(3)] * 2,
            *[planes(4)] * 4,
            planes(6, K + 1),
            *[planes(7)] * 2,
            pltpu.VMEM((2, 3, 8, CY), f32),
            pltpu.VMEM((CX, CY), jnp.int32),
            pltpu.SemaphoreType.DMA((2,)),
            pltpu.SemaphoreType.DMA((N_MESSAGES,)),
            pltpu.SemaphoreType.DMA((N_MESSAGES,)),
        ],
        compiler_params=pltpu.CompilerParams(collective_id=0, has_side_effects=True),
        name="interval",
    )(tracer, velocity, mixing, vertical_mixing, transfer_coef, land_mask)


def solution(mesh):
    return jax.shard_map(
        body,
        mesh=mesh,
        in_specs=(
            P("grp", None, None, "lon", "lat"),
            P("grp", None, None, "lon", "lat"),
            P("grp", None),
            P("grp", None),
            P("lon", "lat"),
            P("lon", "lat"),
        ),
        out_specs=P("grp", None, None, "lon", "lat"),
        check_vma=False,
    )
```

```python
import jax
import jax.numpy as jnp
from jax import lax
from jax.experimental import pallas as pl
from jax.experimental.pallas import tpu as pltpu
from jax.sharding import PartitionSpec as P

SUBSTEPS = 4
OCEAN_SHARE = 0.5
T = 6
K = 8
CX, CY = 32, 128
R0, R1 = 12, 44
ROWS = 56
W = 4
SLOT = 16
OWN = 8
SURFACE, U, V, WET, TRANSFER, PLANES = T, T + T * K, T + T * K + K, 70, 71, 72
MESH = pl.DeviceIdType.MESH


def kernel(tr, vel, mix, vmx, coef, mask, out, f0, f1, f2, f3, sw0, sw1, se0, se1, pw, pe, rw, re, uw, ue, c, cw, ce, hs, msk, lsem, ssem, rsem):
    grp, lon, lat = lax.axis_index("grp"), lax.axis_index("lon"), lax.axis_index("lat")
    nlon, nlat = lax.axis_size("lon"), lax.axis_size("lat")
    ocean = grp == 1

    def exists(di, dj, sign=1):
        ok = None
        for pos, size, d in ((lon, nlon, di * sign), (lat, nlat, dj * sign)):
            if d:
                one = pos < size - 1 if d > 0 else pos > 0
                ok = one if ok is None else jnp.logical_and(ok, one)
        return ok

    def device(dg, di, dj):
        return {"grp": grp if dg == 0 else 1 - grp, "lon": lon + di, "lat": lat + dj}

    def guarded(ok, act):
        if ok is None:
            act()
        else:
            pl.when(ok)(act)

    barrier = pltpu.get_barrier_semaphore()
    places = [(1, a, b) for a in (1, -1) for b in (1, -1)]
    places += [(0, a, b) for a in (1, -1) for b in (1, -1)]
    places += [(1, 1, 0), (1, -1, 0), (1, 0, 1), (1, 0, -1)]
    places += [(1, 0, 0), (0, 0, 1), (0, 0, -1), (0, 1, 0), (0, -1, 0)]
    for where in places:

        def greet(where=where):
            pl.semaphore_signal(barrier, inc=1, device_id=device(*where), device_id_type=MESH)

        guarded(exists(*where[1:]), greet)
    beside = (lon > 0).astype(jnp.int32) + (lon < nlon - 1).astype(jnp.int32)
    along = (lat > 0).astype(jnp.int32) + (lat < nlat - 1).astype(jnp.int32)
    met = 2 * (1 + beside) * (1 + along) - 1

    def level(k):
        return jnp.where(ocean, k, K - 1 - k)

    lo, hi, mid = pl.ds(R0, W), pl.ds(R1 - W, W), pl.ds(R0, CX)
    inlo, inhi = pl.ds(R0 - W, W), pl.ds(R1, W)

    def fetch(k, carry):
        pltpu.make_async_copy(tr.at[0, :, level(k)], f0.at[pl.ds(SURFACE + T * k, T), mid], lsem.at[0]).start()
        pltpu.make_async_copy(vel.at[0, 0, level(k)], f0.at[U + k, mid], lsem.at[0]).start()
        pltpu.make_async_copy(vel.at[0, 1, level(k)], f0.at[V + k, mid], lsem.at[0]).start()
        return carry

    pltpu.make_async_copy(mask, msk, lsem.at[1]).start()
    pltpu.make_async_copy(coef, f0.at[TRANSFER, mid], lsem.at[0]).start()
    lax.fori_loop(0, K, fetch, 0)

    def clear(ref, n, first, count):
        def one(j, carry):
            ref[j, pl.ds(first, count)] = jnp.zeros((count, CY), jnp.float32)
            return carry

        lax.fori_loop(0, n, one, 0)

    @pl.when(lon == 0)
    def _():
        clear(f0, PLANES, R0 - W, W), clear(rw, 4, R0 - W, W), clear(re, 4, R0 - W, W)

    @pl.when(lon == nlon - 1)
    def _():
        clear(f0, PLANES, R1, W), clear(rw, 4, R1, W), clear(re, 4, R1, W)

    @pl.when(lat == 0)
    def _():
        clear(rw, 4, R0 - W, CX + 2 * W)

    @pl.when(lat == nlat - 1)
    def _():
        clear(re, 4, R0 - W, CX + 2 * W)

    lane = lax.broadcasted_iota(jnp.int32, (8, CY), 1)
    sub = lax.broadcasted_iota(jnp.int32, (8, CY), 0)
    zero = jnp.zeros((8, CY), jnp.float32)
    ahead = (lane + W) % CY
    slot = ahead // SLOT
    part = (lane % SLOT) // W
    far_w, far_e = part == 0, part == 1
    def turn(x, shift):
        shift = shift % CY
        return x if shift == 0 else pltpu.roll(x, shift, 1)

    def between(x, a, n):
        return (x >= a) & (x < a + n)

    pltpu.make_async_copy(mask, msk, lsem.at[1]).wait()
    total = pl.ds(0, T * K + 2 * K + 1)
    pltpu.make_async_copy(f0.at[total, mid], f0.at[total, mid], lsem.at[0]).wait()
    f0[WET, mid] = msk[...].astype(jnp.float32)

    def own_edges(ch, rows):
        acc = zero
        for k in range(K):
            x = f0[SURFACE + T * k + ch if ch < T else U + K * (ch - T) + k, rows]
            acc = jnp.where(slot == k, turn(x, SLOT * k + W), acc)
        return acc

    def pack(i, carry):
        rows = pl.ds(R0 + 8 * i, 8)
        west, east = [zero, zero, zero], [zero, zero, zero]
        for ch in range(T + 2):
            x, q, m = own_edges(ch, rows), ch // 4, ch % 4
            west[q] = jnp.where(part == m, turn(x, W * m), west[q])
            east[q] = jnp.where(part == m, turn(x, W * m - W), east[q])
            if ch < T:
                put = between(lane, W * (ch + 2), W)
                west[2] = jnp.where(put, turn(x, W * (ch + 2)), west[2])
                east[2] = jnp.where(put, turn(x, W * (ch + 1)), east[2])
        for j, plane in enumerate((WET, TRANSFER)):
            x, put = f0[plane, rows], between(lane, W * j, W)
            west[2] = jnp.where(put, turn(x, W * (j + 1)), west[2])
            east[2] = jnp.where(put, turn(x, W * j), east[2])
        for q in range(3):
            pw[q, rows], pe[q, rows] = west[q], east[q]
        return carry

    lax.fori_loop(0, CX // 8, pack, 0, unroll=2)

    near, far = [], []
    for dj, p, r in ((1, pw, rw), (-1, pe, re)):
        packs = pl.ds(0, 3)
        near.append(((0, 0, dj), p.at[packs, mid], r.at[packs, mid]))
        near.append(((0, 1, dj), p.at[packs, hi], r.at[packs, inlo]))
        near.append(((0, -1, dj), p.at[packs, lo], r.at[packs, inhi]))
        far.append(((1, 0, dj), p.at[2, mid], r.at[3, mid]))
        far.append(((1, 1, dj), p.at[2, hi], r.at[3, inlo]))
        far.append(((1, -1, dj), p.at[2, lo], r.at[3, inhi]))
    block = pl.ds(SURFACE, PLANES - SURFACE)
    near.append(((0, 1, 0), f0.at[block, hi], f0.at[block, inlo]))
    near.append(((0, -1, 0), f0.at[block, lo], f0.at[block, inhi]))
    surface, other = pl.ds(SURFACE, T), pl.ds(0, T)
    far.append(((1, 1, 0), f0.at[surface, hi], f0.at[other, inlo]))
    far.append(((1, -1, 0), f0.at[surface, lo], f0.at[other, inhi]))
    far.append(((1, 0, 0), f0.at[surface, mid], f0.at[other, mid]))
    messages = near + far

    def remote(n):
        where, src, dst = messages[n]
        return pltpu.make_async_remote_copy(
            src_ref=src, dst_ref=dst, send_sem=ssem.at[n], recv_sem=rsem.at[n], device_id=device(*where), device_id_type=MESH
        )

    def arrived(n):
        guarded(exists(*messages[n][0][1:], sign=-1), lambda: remote(n).wait_recv())

    def sent(n):
        guarded(exists(*messages[n][0][1:]), lambda: remote(n).wait_send())

    pl.semaphore_wait(barrier, met)
    for n in [0, 3, 1, 2, 4, 5, 9, 10, 12, 13, 6, 7, 16, 14, 15, 8, 11]:
        guarded(exists(*messages[n][0][1:]), lambda n=n: remote(n).start())

    def pads(i, carry):
        rows = pl.ds(pl.multiple_of(8 + 8 * i, 8), 8)
        for f in (f1, f2, f3):
            for t in range(T):
                f[t, rows] = zero
                f[T + T * K + t, rows] = zero
        c[5, 0, rows] = zero
        c[5, K, rows] = zero
        return carry

    lax.fori_loop(0, 5, pads, 0)

    def number(k):
        return vmx[0, jnp.where(ocean, k, K - 2 - k)]

    for side, its in enumerate((lane // SLOT, slot)):
        h, up, down = zero, zero, zero
        for k in range(K):
            h = jnp.where(its == k, mix[0, level(k)], h)
            if k > 0:
                up = jnp.where(its == k, number(k - 1), up)
            if k < K - 1:
                down = jnp.where(its == k, number(k), down)
        hs[side, 0], hs[side, 1], hs[side, 2] = h, up, down

    def faces(h, w, wb, wa, u, ub, ua, v):
        wb, wa = w * wb, w * wa
        ws, wn = w * turn(w, 1), w * turn(w, -1)
        sb, sa = 0.25 * (ub + u), 0.25 * (ua + u)
        ss, sn = 0.25 * (turn(v, 1) + v), 0.25 * (turn(v, -1) + v)
        own = 1.0 + (wb * (sb - h) - wa * (sa + h)) + (ws * (ss - h) - wn * (sn + h))
        return own, wb * (sb + h), wa * (h - sa), ws * (ss + h), wn * (h - sn)

    def opening(o, wet, beyond=False):
        row = o + sub
        shut = ((row < R0) & (lon == 0)) | ((row >= R1) & (lon == nlon - 1)) | beyond
        return jnp.where(shut, 0.0, jnp.where(ocean, wet, 1.0))

    def coefficients(o, rows):
        before, after = pl.ds(o - 1, 8), pl.ds(o + 1, 8)
        w, wb, wa = opening(o, f0[WET, rows]), opening(o - 1, f0[WET, before]), opening(o + 1, f0[WET, after])
        above = None
        for k in range(K):
            u, ub, ua = f0[U + k, rows], f0[U + k, before], f0[U + k, after]
            own, *others = faces(mix[0, level(k)], w, wb, wa, u, ub, ua, f0[V + k, rows])
            for j in range(4):
                c[1 + j, k, rows] = others[j]
            if k > 0:
                own = own - above
            if k < K - 1:
                above = w * number(k)
                c[5, k + 1, rows] = above
                own = own - above
            c[0, k, rows] = own

    def inner(i, carry):
        @pl.when(i == 3)
        def _():
            for n in range(len(near)):
                sent(n)
            for n in range(len(near)):
                arrived(n)

        o = pl.multiple_of(jnp.where(i < 3, 16 + 8 * i, 8 + 32 * (i - 3)), 8)
        rows = pl.ds(o, 8)
        for ch in range(T + 2):
            x = own_edges(ch, rows)
            if ch < T:
                sw0[ch, rows], se0[ch, rows] = x, x
            else:
                uw[ch - T, rows], ue[ch - T, rows] = x, x
        coefficients(o, rows)
        return carry

    lax.fori_loop(0, 5, inner, 0)

    share = jnp.where(ocean, OCEAN_SHARE, 1.0)

    def repeat(x):
        x = x + turn(x, SLOT)
        x = x + turn(x, 2 * SLOT)
        return x + turn(x, 4 * SLOT)

    def outer(i, carry):
        o = 8 + 8 * i
        rows = pl.ds(pl.multiple_of(o, 8), 8)
        for ch in range(T + 2):
            q, m = ch // 4, ch % 4
            west, east = (sw0.at[ch], se0.at[ch]) if ch < T else (uw.at[ch - T], ue.at[ch - T])
            west[rows] = jnp.where(far_w, turn(rw[q, rows], -W * m), west[rows])
            east[rows] = jnp.where(far_e, turn(re[q, rows], W - W * m), east[rows])
        wet, transfer = turn(f0[WET, rows], W), turn(f0[TRANSFER, rows], W)
        first = slot == 0
        for r, fields, far, at, beyond in ((rw, uw, far_w & first, 0, lat == 0), (re, ue, far_e & first, W, lat == nlat - 1)):
            ours = between(lane, W, 2 * W) if r is rw else between(ahead, 0, 2 * W)
            near_wet = jnp.where(far, turn(r[2, rows], at), jnp.where(ours, wet, 0.0))
            gain = jnp.where(far, turn(r[2, rows], at - W), jnp.where(ours, transfer, 0.0))
            fields[2, rows] = opening(o, repeat(near_wet), (far_w if r is rw else far_e) & beyond)
            fields[3, rows] = share * gain * near_wet
        return carry

    lax.fori_loop(0, 5, outer, 0)

    def edges(i, carry):
        o = 8 + 8 * i
        rows, before, after = pl.ds(pl.multiple_of(o, 8), 8), pl.ds(o - 1, 8), pl.ds(o + 1, 8)
        for side, (fields, cs) in enumerate(((uw, cw), (ue, ce))):
            w = fields[2, rows]
            up, down = w * hs[side, 1], w * hs[side, 2]
            u = [fields[0, r] for r in (rows, before, after)]
            own, *others = faces(hs[side, 0], w, fields[2, before], fields[2, after], *u, fields[1, rows])
            for j, x in enumerate((own - up - down, *others, up, down)):
                cs[j, rows] = x
        return carry

    lax.fori_loop(0, 5, edges, 0)

    def stencil(src, k, o):
        rows, before, after = pl.ds(o, 8), pl.ds(o - 1, 8), pl.ds(o + 1, 8)
        co, cb, ca, cs, cn = (c[j, k, rows] for j in range(5))
        up, down = c[5, k, rows], c[5, k + 1, rows]
        for t in range(T):
            p = SURFACE + T * k + t
            x = src[p, rows]
            y = co * x + cb * src[p, before] + ca * src[p, after]
            y = y + (cs * turn(x, 1) + cn * turn(x, -1))
            yield t, y + (up * src[p - T, rows] + down * src[p + T, rows])

    def substep(src, dst, first, pairs):
        def one(n, carry):
            for k in (first + 2 * n, first + 2 * n + 1):
                for i in range(5):
                    o = 8 + 8 * i
                    for t, y in stencil(src, k, o):
                        dst[SURFACE + T * k + t, pl.ds(o, 8)] = y
            return carry

        lax.fori_loop(0, pairs, one, 0)

    def strip_substep(west, east, wnext, enext):
        if True:
            for i in range(5):
                o = 8 + 8 * i
                rows, before, after = pl.ds(o, 8), pl.ds(o - 1, 8), pl.ds(o + 1, 8)
                for src, dst, cs in ((west, wnext, cw), (east, enext, ce)):
                    co, cb, ca, cl, cr, up, down = (cs[j, rows] for j in range(7))
                    for t in range(T):
                        x = src[t, rows]
                        y = co * x + cb * src[t, before] + ca * src[t, after]
                        dst[t, rows] = y + (cl * turn(x, 1) + cr * turn(x, -1))
            for i in range(5):
                o = 8 + 8 * i
                rows, before, after = pl.ds(o, 8), pl.ds(o - 1, 8), pl.ds(o + 1, 8)
                for src, dst, cs in ((west, wnext, cw), (east, enext, ce)):
                    co, cb, ca, cl, cr, up, down = (cs[j, rows] for j in range(7))
                    for t in range(T):
                        x = src[t, rows]
                        dst[t, rows] = dst[t, rows] + (up * turn(x, SLOT) + down * turn(x, -SLOT))

    def finish(n, carry):
        stale = (lane < W) | (lane >= CY - W)
        for k in (2 * n, 2 * n + 1):
            for i in range(CX // 8):
                o = R0 + 8 * i
                for t, y in stencil(f3, k, o):
                    fresh = jnp.where(far_w, se0[t, pl.ds(o, 8)], sw0[t, pl.ds(o, 8)])
                    fresh = pltpu.roll(fresh, CY - W - SLOT * k, 1)
                    out[0, t, level(k), pl.ds(8 * i, 8)] = jnp.where(stale, fresh, y)
        return carry

    def exchange(i, carry):
        rows = pl.ds(pl.multiple_of(8 + 8 * i, 8), 8)
        gain = share * f0[TRANSFER, rows] * f0[WET, rows]
        for t in range(T):
            x = f0[SURFACE + t, rows]
            f0[SURFACE + t, rows] = x + gain * (f0[t, rows] - x)
        for t in range(T):
            theirs = turn(f0[t, rows], W)
            west = jnp.where(far_w, turn(rw[3, rows], -W * (t + 2)), theirs)
            east = jnp.where(far_e, turn(re[3, rows], -W * (t + 1)), theirs)
            for s, fields, x in ((sw0, uw, west), (se0, ue, east)):
                s[t, rows] = s[t, rows] + fields[3, rows] * (x - s[t, rows])
        return carry

    def phase(late, carry):
        @pl.when(late == 1)
        def _():
            for n in range(len(near), len(messages)):
                sent(n)
            for n in range(len(near), len(messages)):
                arrived(n)
            lax.fori_loop(0, 5, exchange, 0)

        early = 1 - late
        substep(f0, f1, 2 * early, 1 + 2 * early)
        substep(f1, f2, 2 * early, 2 + early)
        substep(f2, f3, 4 * early, 2)
        return carry

    lax.fori_loop(0, 2, phase, 0)

    def strips(j, carry):
        strip_substep(sw0, se0, sw1, se1)
        strip_substep(sw1, se1, sw0, se0)
        return carry

    lax.fori_loop(0, SUBSTEPS // 2, strips, 0)
    lax.fori_loop(0, K // 2, finish, 0)


N_MESSAGES = 17


def body(tracer, velocity, mixing, vertical_mixing, transfer_coef, land_mask):
    f32 = jnp.float32
    anywhere = pl.BlockSpec(memory_space=pl.ANY)
    scalars = pl.BlockSpec(memory_space=pltpu.SMEM)

    def planes(*n):
        return pltpu.VMEM((*n, ROWS, CY), f32)

    return pl.pallas_call(
        kernel,
        out_shape=pltpu.VMEM(tracer.shape, f32),
        in_specs=[anywhere, anywhere, scalars, scalars, anywhere, anywhere],
        out_specs=pl.BlockSpec(memory_space=pltpu.VMEM),
        scratch_shapes=[
            planes(PLANES),
            *[planes(T * (K + 2))] * 3,
            *[planes(T)] * 4,
            *[planes(3)] * 2,
            *[planes(4)] * 4,
            planes(6, K + 1),
            *[planes(7)] * 2,
            pltpu.VMEM((2, 3, 8, CY), f32),
            pltpu.VMEM((CX, CY), jnp.int32),
            pltpu.SemaphoreType.DMA((2,)),
            pltpu.SemaphoreType.DMA((N_MESSAGES,)),
            pltpu.SemaphoreType.DMA((N_MESSAGES,)),
        ],
        compiler_params=pltpu.CompilerParams(collective_id=0, has_side_effects=True),
        name="interval",
    )(tracer, velocity, mixing, vertical_mixing, transfer_coef, land_mask)


def solution(mesh):
    return jax.shard_map(
        body,
        mesh=mesh,
        in_specs=(
            P("grp", None, None, "lon", "lat"),
            P("grp", None, None, "lon", "lat"),
            P("grp", None),
            P("grp", None),
            P("lon", "lat"),
            P("lon", "lat"),
        ),
        out_specs=P("grp", None, None, "lon", "lat"),
        check_vma=False,
    )
```
